128 devices in a mesh: fsdp: 32 (over x, z, y_lo), tensor: 4 (over y_hi, core).
Axes of the slice: x: 4, y: 4 (y_hi: 2, y_lo: 2; y = y_hi * 2 + y_lo), z: 4, core: 2. Of those that a mesh axis runs over, the one named last changes fastest.
Arguments:
- hidden_in: bfloat16 [16384, 5120], P('fsdp', 'tensor'), may hold values from -80 to 80
- norm_gain: bfloat16 [5120], replicated, may hold values from 0.099609375 to 1.8984375
- query_weight: bfloat16 [5120, 5120], P(('fsdp', 'tensor')), may hold values from -0.078125 to 0.078125
- key_weight: bfloat16 [5120, 1024], P(('fsdp', 'tensor')), may hold values from -0.078125 to 0.078125
- value_weight: bfloat16 [5120, 1024], P(('fsdp', 'tensor')), may hold values from -0.078125 to 0.078125
- out_weight: bfloat16 [5120, 5120], P(('fsdp', 'tensor')), may hold values from -0.078125 to 0.078125
- query_bias: bfloat16 [5120], P('tensor'), may hold values from -10.5 to 10.5
- key_bias: bfloat16 [1024], P('tensor'), may hold values from -5.5 to 5.5
- value_bias: bfloat16 [1024], P('tensor'), may hold values from -3 to 3
- span_start: int32 [64], P('fsdp'), may hold values from 0 to 3839
- span_length: int32 [64], P('fsdp'), may hold values from 64 to 256, as said below
Outputs:
- attention_out: bfloat16 [16384, 5120], P('fsdp', 'tensor')
- key_cache: bfloat16 [16384, 1024], P('fsdp', 'tensor')
- value_cache: bfloat16 [16384, 1024], P('fsdp', 'tensor')
The draws below stay inside these ranges and needn't reach their ends.
Inputs may be any that keep to these rules, and one draw needn't show every extreme that they name: `span_length`: the spans of the first rollout group are all full.
All inputs are finite; a program needn't handle non-finite values.
Results may differ from the reference program's by a relative error of at most 0.0065.
The reference program's roundings to bfloat16 on the way count: a program that leaves them out, or rounds other values in their place, can miss the bound.
Values may be sent and summed in bfloat16 or wider, within the bound.
No kernel may reach another device: no remote copies, remote signals or barrier semaphores. Data moves between devices by JAX's collectives and lax.ppermute only.
A program may use at most 128 MiB of HBM per device.

```python
import jax
import jax.numpy as jnp
from jax import lax

D = 5120
HEADS = 40
KV_HEADS = 8
HEAD = 128
SPAN = 256
SEQS = 2
MAXPOS = 4096
SPANS = 64
TOKENS = 16384


def draw_hidden_in(key, part):
    base_key = jax.random.fold_in(key, 101)
    row_key = jax.random.fold_in(key, 102)
    column_key = jax.random.fold_in(key, 103)
    base = jnp.clip(jax.random.normal(base_key, (TOKENS, D), jnp.float32), -4.0, 4.0)
    row_scale = 0.3 * jnp.exp(jax.random.uniform(row_key, (TOKENS, 1), jnp.float32) * jnp.log(10.0))
    ramp = jnp.exp(jnp.log(10.0) * (jnp.arange(D, dtype=jnp.float32) / D - 0.5))
    jitter = jnp.exp(jax.random.uniform(column_key, (D,), jnp.float32) * jnp.log(2.0))
    return (base * row_scale * (ramp * jitter)[None, :]).astype(jnp.bfloat16)


def bias_pair(key):
    query_part = 0.5 * jnp.clip(jax.random.normal(jax.random.fold_in(key, 205), (HEADS, HEAD), jnp.float32), -3.0, 3.0)
    key_part = 0.5 * jnp.clip(jax.random.normal(jax.random.fold_in(key, 206), (KV_HEADS, HEAD), jnp.float32), -3.0, 3.0)
    return (query_part.reshape(HEADS * HEAD), key_part.reshape(KV_HEADS * HEAD))


def draw_query_bias(key, part):
    return bias_pair(key)[0].astype(jnp.bfloat16)


def draw_key_bias(key, part):
    return bias_pair(key)[1].astype(jnp.bfloat16)


def draw_span_length(key, part):
    lengths = jax.random.randint(jax.random.fold_in(key, 301), (SPANS,), SPAN // 4, SPAN + 1, dtype=jnp.int32)
    return lengths.at[:SEQS].set(SPAN)


def set_ends(values, own_key, least, top_value):
    longest = values.shape.index(max(values.shape))
    spots = []
    for shift in (0, 1):
        where = [jax.random.randint(jax.random.fold_in(own_key, axis), (), 0, length) for axis, length in enumerate(values.shape)]
        where[longest] = (where[longest] + shift) % values.shape[longest]
        spots.append(tuple(where))
    return values.at[spots[0]].set(least).at[spots[1]].set(top_value)


def steps_of(own_key, dims, cuts, least, largest):
    loudness = 1.0
    for position, shards_of in cuts:
        heights = jax.random.uniform(jax.random.fold_in(jax.random.fold_in(own_key, 6), position), (shards_of,), jnp.float32, least / len(cuts), largest / len(cuts))
        loudness = loudness * jnp.repeat(jnp.exp(heights), dims[position] // shards_of).reshape((-1,) + (1,) * (len(dims) - 1 - position))
    return loudness


def bell_draw(rng, dims, width, limit, split=(), held_as=jnp.bfloat16):
    gain = steps_of(rng, dims, split, -0.22, 0.18) if split else 1.0
    values = jax.random.normal(rng, dims, jnp.float32) * width * gain
    return jnp.minimum(jnp.maximum(values, -limit), limit).astype(held_as)


def setup_inputs(seed: int = 0) -> dict:
    arg_keys = jax.random.split(jax.random.key(seed), 12)
    hidden_in = draw_hidden_in(jax.random.fold_in(arg_keys[11], 71), 0)
    norm_gain = jnp.clip(1.0 + 0.18 * jax.random.normal(arg_keys[1], (D,), jnp.float32), 0.099609375, 1.8984375).astype(jnp.bfloat16)
    query_weight = bell_draw(arg_keys[2], (D, HEADS * HEAD), D ** -0.5, 0.078125, ((0, 128),))
    key_weight = bell_draw(arg_keys[3], (D, KV_HEADS * HEAD), D ** -0.5, 0.078125, ((0, 128),))
    value_weight = bell_draw(arg_keys[4], (D, KV_HEADS * HEAD), D ** -0.5, 0.078125, ((0, 128),))
    out_weight = bell_draw(arg_keys[5], (HEADS * HEAD, D), (HEADS * HEAD) ** -0.5, 0.078125, ((0, 128),))
    query_bias = draw_query_bias(jax.random.fold_in(arg_keys[11], 71), 0)
    key_bias = draw_key_bias(jax.random.fold_in(arg_keys[11], 71), 0)
    value_bias = bell_draw(arg_keys[8], (KV_HEADS * HEAD,), 0.5, 3.0, ((0, 4),))
    span_start = set_ends(jax.random.randint(arg_keys[9], (SPANS,), 0, MAXPOS - SPAN), jax.random.fold_in(arg_keys[9], 1), 0, (MAXPOS - SPAN) - 1).astype(jnp.int32)
    span_length = draw_span_length(jax.random.fold_in(arg_keys[11], 71), 0)
    return {"hidden_in": hidden_in, "norm_gain": norm_gain, "query_weight": query_weight, "key_weight": key_weight, "value_weight": value_weight, "out_weight": out_weight, "query_bias": query_bias, "key_bias": key_bias, "value_bias": value_bias, "span_start": span_start, "span_length": span_length}


rope_base = 1000000.0
epsilon = 1e-06

def rotate(entries, cosine, sine):
    half = entries.shape[-1] // 2
    first = entries[..., :half]
    second = entries[..., half:]
    return jnp.concatenate([first * cosine - second * sine, second * cosine + first * sine], axis=-1)

def angles(span_start, span_size):
    positions = span_start[:, None] + jnp.arange(span_size, dtype=jnp.int32)[None, :]
    inverse = 1.0 / rope_base ** (jnp.arange(0, HEAD, 2, dtype=jnp.float32) / HEAD)
    phase = positions.reshape(-1).astype(jnp.float32)[:, None] * inverse[None, :]
    return (jnp.cos(phase)[:, None, :], jnp.sin(phase)[:, None, :])

def reference(hidden_in, norm_gain, query_weight, key_weight, value_weight, out_weight, query_bias, key_bias, value_bias, span_start, span_length):
    source = hidden_in.astype(jnp.float32)
    inverse_rms = lax.rsqrt(lax.optimization_barrier(jnp.mean(source * source, axis=-1, keepdims=True)) + epsilon)
    normed = (source * inverse_rms * norm_gain.astype(jnp.float32)).astype(jnp.bfloat16)
    query = jnp.dot(normed, query_weight, preferred_element_type=jnp.float32) + query_bias.astype(jnp.float32)
    keys = jnp.dot(normed, key_weight, preferred_element_type=jnp.float32) + key_bias.astype(jnp.float32)
    values = jnp.dot(normed, value_weight, preferred_element_type=jnp.float32) + value_bias.astype(jnp.float32)
    cosine, sine = angles(span_start, SPAN)
    query = rotate(query.reshape(TOKENS, HEADS, HEAD), cosine, sine).astype(jnp.bfloat16)
    keys = rotate(keys.reshape(TOKENS, KV_HEADS, HEAD), cosine, sine)
    live = (jnp.arange(SPAN, dtype=jnp.int32)[None, :] < span_length[:, None]).reshape(TOKENS, 1, 1)
    key_cache = jnp.where(live, keys, 0.0).astype(jnp.bfloat16)
    value_cache = jnp.where(live, values.reshape(TOKENS, KV_HEADS, HEAD), 0.0).astype(jnp.bfloat16)
    groups = HEADS // KV_HEADS

    def attend(item):
        query_block, key_block, value_block, length = item
        query_wide = query_block.astype(jnp.float32).reshape(SPAN, KV_HEADS, groups, HEAD)
        scores = jnp.einsum('qkgd,tkd->kgqt', query_wide, key_block.astype(jnp.float32)) * HEAD ** (-0.5)
        rows = jnp.arange(SPAN, dtype=jnp.int32)[:, None]
        columns = jnp.arange(SPAN, dtype=jnp.int32)[None, :]
        allowed = (columns <= rows) & (columns < length)
        scores = jnp.where(allowed, scores, -1e+30)
        highest = lax.optimization_barrier(jnp.max(scores, axis=-1, keepdims=True))
        raised = jnp.exp(scores - highest)
        probs = (raised / lax.optimization_barrier(jnp.sum(raised, axis=-1, keepdims=True))).astype(jnp.bfloat16)
        mixed = jnp.einsum('kgqt,tkd->qkgd', probs.astype(jnp.float32), value_block.astype(jnp.float32))
        return mixed.reshape(SPAN, HEADS * HEAD).astype(jnp.bfloat16)
    attended = lax.map(attend, (query.reshape(SPANS, SPAN, HEADS, HEAD), key_cache.reshape(SPANS, SPAN, KV_HEADS, HEAD), value_cache.reshape(SPANS, SPAN, KV_HEADS, HEAD), span_length))
    attended = attended.reshape(TOKENS, HEADS * HEAD)
    attention_out = jnp.dot(attended, out_weight, preferred_element_type=jnp.float32).astype(jnp.bfloat16)
    return (attention_out, key_cache.reshape(TOKENS, KV_HEADS * HEAD), value_cache.reshape(TOKENS, KV_HEADS * HEAD))
```

```python
import jax
import jax.numpy as jnp
from jax import lax
from jax.sharding import PartitionSpec as P

HEADS = 40
KV_HEADS = 8
HEAD = 128


rope_base = 1000000.0
epsilon = 1e-06


def rotate(entries, cosine, sine):
    half = entries.shape[-1] // 2
    first = entries[..., :half]
    second = entries[..., half:]
    return jnp.concatenate(
        [first * cosine - second * sine, second * cosine + first * sine], axis=-1
    )


def angles(span_start, span_size):
    positions = span_start[:, None] + jnp.arange(span_size, dtype=jnp.int32)[None, :]
    inverse = 1.0 / rope_base ** (jnp.arange(0, HEAD, 2, dtype=jnp.float32) / HEAD)
    phase = positions.reshape(-1).astype(jnp.float32)[:, None] * inverse[None, :]
    return (jnp.cos(phase)[:, None, :], jnp.sin(phase)[:, None, :])


def local(
    hidden_in,
    norm_gain,
    query_weight,
    key_weight,
    value_weight,
    out_weight,
    query_bias,
    key_bias,
    value_bias,
    span_start,
    span_length,
):
    slices = lax.axis_size("tensor")
    members = lax.axis_size("fsdp")
    token_rows = hidden_in.shape[0]
    local_spans = span_start.shape[0]
    span_size = token_rows // local_spans
    query_cols = query_weight.shape[1] // slices
    key_cols = key_weight.shape[1] // slices
    learner_rows = query_weight.shape[0]
    gathered = lax.all_gather(hidden_in, "tensor", axis=1, tiled=True)
    source = gathered.astype(jnp.float32)
    inverse_rms = lax.rsqrt(jnp.mean(source * source, axis=-1, keepdims=True) + epsilon)
    normed = (source * inverse_rms * norm_gain.astype(jnp.float32)).astype(jnp.bfloat16)
    joined = jnp.concatenate(
        [
            query_weight.reshape(learner_rows, slices, query_cols),
            key_weight.reshape(learner_rows, slices, key_cols),
            value_weight.reshape(learner_rows, slices, key_cols),
        ],
        axis=2,
    )
    joined_cols = joined.shape[2]
    exchanged = lax.all_to_all(joined, "tensor", split_axis=1, concat_axis=0, tiled=True)
    arrived = lax.all_gather(
        exchanged.reshape(slices * learner_rows, joined_cols), "fsdp", axis=0, tiled=True
    )
    projected = jnp.dot(
        normed, arrived.reshape(-1, joined_cols), preferred_element_type=jnp.float32
    )
    query = projected[:, :query_cols] + query_bias.astype(jnp.float32)
    keys = projected[:, query_cols : query_cols + key_cols] + key_bias.astype(jnp.float32)
    values = projected[:, query_cols + key_cols :] + value_bias.astype(jnp.float32)
    local_heads = query_cols // HEAD
    local_kv = key_cols // HEAD
    groups = HEADS // KV_HEADS
    cosine, sine = angles(span_start, span_size)
    query = rotate(query.reshape(token_rows, local_heads, HEAD), cosine, sine).astype(jnp.bfloat16)
    keys = rotate(keys.reshape(token_rows, local_kv, HEAD), cosine, sine)
    live = (jnp.arange(span_size, dtype=jnp.int32)[None, :] < span_length[:, None]).reshape(
        token_rows, 1, 1
    )
    key_cache = jnp.where(live, keys, 0.0).astype(jnp.bfloat16)
    value_cache = jnp.where(live, values.reshape(token_rows, local_kv, HEAD), 0.0).astype(
        jnp.bfloat16
    )
    query_blocks = query.reshape(local_spans, span_size, local_kv, groups, HEAD)
    key_blocks = key_cache.reshape(local_spans, span_size, local_kv, HEAD)
    value_blocks = value_cache.reshape(local_spans, span_size, local_kv, HEAD)
    scores = jnp.einsum(
        "sqkgd,stkd->skgqt", query_blocks, key_blocks, preferred_element_type=jnp.float32
    ) * HEAD ** (-0.5)
    rows = jnp.arange(span_size, dtype=jnp.int32)[:, None]
    columns = jnp.arange(span_size, dtype=jnp.int32)[None, :]
    allowed = (columns <= rows)[None] & (columns[None] < span_length[:, None, None])
    scores = jnp.where(allowed[:, None, None], scores, -1e30)
    highest = jnp.max(scores, axis=-1, keepdims=True)
    raised = jnp.exp(scores - highest)
    probs = (raised / jnp.sum(raised, axis=-1, keepdims=True)).astype(jnp.bfloat16)
    mixed = jnp.einsum("skgqt,stkd->sqkgd", probs, value_blocks, preferred_element_type=jnp.float32)
    attended = mixed.reshape(token_rows, local_heads * HEAD).astype(jnp.bfloat16)
    all_heads = lax.all_gather(attended, "tensor", axis=1, tiled=True)
    out_rows_local = out_weight.shape[0]
    out_cols = out_weight.shape[1] // slices
    out_block = out_weight.reshape(out_rows_local, slices, out_cols)
    exchanged_out = lax.all_to_all(out_block, "tensor", split_axis=1, concat_axis=0, tiled=True)
    arrived_out = lax.all_gather(
        exchanged_out.reshape(slices * out_rows_local, out_cols), "fsdp", axis=0, tiled=True
    )
    combined = jnp.dot(
        all_heads, arrived_out.reshape(-1, out_cols), preferred_element_type=jnp.float32
    )
    attention_out = combined.astype(jnp.bfloat16)
    return (
        attention_out,
        key_cache.reshape(token_rows, local_kv * HEAD),
        value_cache.reshape(token_rows, local_kv * HEAD),
    )


def solution(mesh):
    placed = (
        P("fsdp", "tensor"),
        P(),
        P(("fsdp", "tensor"), None),
        P(("fsdp", "tensor"), None),
        P(("fsdp", "tensor"), None),
        P(("fsdp", "tensor"), None),
        P("tensor"),
        P("tensor"),
        P("tensor"),
        P("fsdp"),
        P("fsdp"),
    )
    return jax.shard_map(
        local,
        mesh=mesh,
        in_specs=placed,
        out_specs=(P("fsdp", "tensor"), P("fsdp", "tensor"), P("fsdp", "tensor")),
        check_vma=False,
    )
```

```python
import jax
import jax.numpy as jnp
import numpy as np
from jax import lax
from jax.sharding import Mesh
from jax.sharding import PartitionSpec as P

HEADS = 40
KV_HEADS = 8
HEAD = 128


rope_base = 1000000.0
epsilon = 1e-06

ROW_AXES = ("x", "z", "ylo")
COL_AXES = ("yhi", "core")


def rotate(entries, cosine, sine):
    half = entries.shape[-1] // 2
    first = entries[..., :half]
    second = entries[..., half:]
    return jnp.concatenate(
        [first * cosine - second * sine, second * cosine + first * sine], axis=-1
    )


def angles(span_start, span_size):
    positions = span_start[:, None] + jnp.arange(span_size, dtype=jnp.int32)[None, :]
    inverse = 1.0 / rope_base ** (jnp.arange(0, HEAD, 2, dtype=jnp.float32) / HEAD)
    phase = positions.reshape(-1).astype(jnp.float32)[:, None] * inverse[None, :]
    return (jnp.cos(phase)[:, None, :], jnp.sin(phase)[:, None, :])


def shift(value, axis, step):
    n = lax.axis_size(axis)
    return lax.ppermute(value, axis, [(j, (j + step) % n) for j in range(n)])


def gather_axis(blocks, axis):
    n = lax.axis_size(axis)
    if n == 1:
        return blocks[None]
    if n == 2:
        return jnp.stack([blocks, shift(blocks, axis, 1)])
    assert n == 4
    from_prev = shift(blocks, axis, 1)
    from_next = shift(blocks, axis, -1)
    half = blocks.shape[-1] // 2
    far_a = shift(from_next[..., :half], axis, -1)
    far_b = shift(from_prev[..., half:], axis, 1)
    far = jnp.concatenate([far_a, far_b], axis=-1)
    return jnp.stack([blocks, from_next, far, from_prev])


def exchange_slices(local_rows):
    yhi = lax.axis_index("yhi")
    core = lax.axis_index("core")
    own = yhi * 2 + core
    pick = lambda t: lax.dynamic_index_in_dim(local_rows, t, axis=1, keepdims=False)
    mine = pick(own)
    from_core = shift(pick(yhi * 2 + (1 - core)), "core", 1)
    from_yhi = shift(pick((1 - yhi) * 2 + core), "yhi", 1)
    diag = 3 - own
    from_diag = lax.ppermute(
        pick(diag), ("yhi", "core"), [(j, 3 - j) for j in range(4)]
    )
    parts = []
    for p in range(4):
        k = p ^ own
        parts.append(
            jnp.where(k == 0, mine, jnp.where(k == 1, from_core, jnp.where(k == 2, from_yhi, from_diag)))
        )
    return jnp.concatenate(parts, axis=0)


def gather_first(block):
    paired = gather_axis(block, "ylo")
    half = block.shape[0] // 2
    return gather_axis(paired[:, :half], "x"), gather_axis(paired[:, half:], "z")


def gather_second(first):
    return gather_axis(first[0], "z"), gather_axis(first[1], "x")


def relative_columns(values, rows):
    tokens = values.shape[0]
    nx, nz, nl = (lax.axis_size(a) for a in ROW_AXES)
    ix, iz, il = (lax.axis_index(a) for a in ROW_AXES)
    grid = values.reshape(tokens, nx, nz, nl, rows)
    grid = jnp.roll(grid, -ix, axis=1)
    grid = jnp.roll(grid, -iz, axis=2)
    grid = jnp.roll(grid, -il, axis=3)
    half = rows // 2
    part_a = jnp.transpose(grid[..., :half], (0, 2, 1, 3, 4)).reshape(tokens, -1)
    part_b = grid[..., half:].reshape(tokens, -1)
    return part_a, part_b


def project(values, portions, rows):
    portion_a, portion_b = portions
    cols = portion_a.shape[-1]
    part_a, part_b = relative_columns(values, rows)
    first = jnp.dot(part_a, portion_a.reshape(-1, cols), preferred_element_type=jnp.float32)
    second = jnp.dot(part_b, portion_b.reshape(-1, cols), preferred_element_type=jnp.float32)
    return first + second


def local(
    hidden_in,
    norm_gain,
    query_weight,
    key_weight,
    value_weight,
    out_weight,
    query_bias,
    key_bias,
    value_bias,
    span_start,
    span_length,
):
    slices = lax.axis_size(COL_AXES)
    token_rows = hidden_in.shape[0]
    local_spans = span_start.shape[0]
    span_size = token_rows // local_spans
    query_cols = query_weight.shape[1] // slices
    key_cols = key_weight.shape[1] // slices
    learner_rows = query_weight.shape[0]
    block_rows = slices * learner_rows
    joined = jnp.concatenate(
        [
            query_weight.reshape(learner_rows, slices, query_cols),
            key_weight.reshape(learner_rows, slices, key_cols),
            value_weight.reshape(learner_rows, slices, key_cols),
        ],
        axis=2,
    )
    joined_block = exchange_slices(joined)
    qkv_portions = gather_second(gather_first(joined_block))
    qkv_portions, out_weight = lax.optimization_barrier((qkv_portions, out_weight))
    out_rows_local = out_weight.shape[0]
    out_cols = out_weight.shape[1] // slices
    out_block = exchange_slices(out_weight.reshape(out_rows_local, slices, out_cols))
    out_first = gather_first(out_block)
    gathered = lax.all_gather(hidden_in, COL_AXES, axis=1, tiled=True)
    source = gathered.astype(jnp.float32)
    inverse_rms = lax.rsqrt(jnp.mean(source * source, axis=-1, keepdims=True) + epsilon)
    normed = (source * inverse_rms * norm_gain.astype(jnp.float32)).astype(jnp.bfloat16)
    projected = project(normed, qkv_portions, block_rows)
    query = projected[:, :query_cols] + query_bias.astype(jnp.float32)
    keys = projected[:, query_cols : query_cols + key_cols] + key_bias.astype(jnp.float32)
    values = projected[:, query_cols + key_cols :] + value_bias.astype(jnp.float32)
    local_heads = query_cols // HEAD
    local_kv = key_cols // HEAD
    groups = HEADS // KV_HEADS
    cosine, sine = angles(span_start, span_size)
    query = rotate(query.reshape(token_rows, local_heads, HEAD), cosine, sine).astype(jnp.bfloat16)
    keys = rotate(keys.reshape(token_rows, local_kv, HEAD), cosine, sine)
    live = (jnp.arange(span_size, dtype=jnp.int32)[None, :] < span_length[:, None]).reshape(
        token_rows, 1, 1
    )
    key_cache = jnp.where(live, keys, 0.0).astype(jnp.bfloat16)
    value_cache = jnp.where(live, values.reshape(token_rows, local_kv, HEAD), 0.0).astype(
        jnp.bfloat16
    )
    query, key_cache, value_cache, out_first = lax.optimization_barrier(
        (query, key_cache, value_cache, out_first)
    )
    out_portions = gather_second(out_first)
    query_blocks = query.reshape(local_spans, span_size, local_kv, groups, HEAD)
    key_blocks = key_cache.reshape(local_spans, span_size, local_kv, HEAD)
    value_blocks = value_cache.reshape(local_spans, span_size, local_kv, HEAD)
    scores = jnp.einsum(
        "sqkgd,stkd->skgqt", query_blocks, key_blocks, preferred_element_type=jnp.float32
    ) * HEAD ** (-0.5)
    rows = jnp.arange(span_size, dtype=jnp.int32)[:, None]
    columns = jnp.arange(span_size, dtype=jnp.int32)[None, :]
    allowed = (columns <= rows)[None] & (columns[None] < span_length[:, None, None])
    scores = jnp.where(allowed[:, None, None], scores, -1e30)
    highest = jnp.max(scores, axis=-1, keepdims=True)
    raised = jnp.exp(scores - highest)
    probs = (raised / jnp.sum(raised, axis=-1, keepdims=True)).astype(jnp.bfloat16)
    mixed = jnp.einsum("skgqt,stkd->sqkgd", probs, value_blocks, preferred_element_type=jnp.float32)
    attended = mixed.reshape(token_rows, local_heads * HEAD).astype(jnp.bfloat16)
    all_heads = lax.all_gather(attended, COL_AXES, axis=1, tiled=True)
    combined = project(all_heads, out_portions, block_rows)
    attention_out = combined.astype(jnp.bfloat16)
    return (
        attention_out,
        key_cache.reshape(token_rows, local_kv * HEAD),
        value_cache.reshape(token_rows, local_kv * HEAD),
    )


def physical_mesh(mesh):
    members = mesh.shape["fsdp"]
    slices = mesh.shape["tensor"]
    shape = (4, members // 8, 2, slices // 2, 2)
    return Mesh(np.asarray(mesh.devices).reshape(shape), ROW_AXES + COL_AXES)


def solution(mesh):
    fine = physical_mesh(mesh)
    rows = ROW_AXES
    both = ROW_AXES + COL_AXES
    placed = (
        P(rows, COL_AXES),
        P(),
        P(both, None),
        P(both, None),
        P(both, None),
        P(both, None),
        P(COL_AXES),
        P(COL_AXES),
        P(COL_AXES),
        P(rows),
        P(rows),
    )
    return jax.shard_map(
        local,
        mesh=fine,
        in_specs=placed,
        out_specs=(P(rows, COL_AXES), P(rows, COL_AXES), P(rows, COL_AXES)),
        check_vma=False,
    )
```

```python
import jax
import jax.numpy as jnp
import numpy as np
from jax import lax
from jax.sharding import Mesh
from jax.sharding import PartitionSpec as P

HEADS = 40
KV_HEADS = 8
HEAD = 128


rope_base = 1000000.0
epsilon = 1e-06

ROW_AXES = ("x", "z", "ylo")
COL_AXES = ("yhi", "core")


def rotate(entries, cosine, sine):
    half = entries.shape[-1] // 2
    first = entries[..., :half]
    second = entries[..., half:]
    return jnp.concatenate(
        [first * cosine - second * sine, second * cosine + first * sine], axis=-1
    )


def angles(span_start, span_size):
    positions = span_start[:, None] + jnp.arange(span_size, dtype=jnp.int32)[None, :]
    inverse = 1.0 / rope_base ** (jnp.arange(0, HEAD, 2, dtype=jnp.float32) / HEAD)
    phase = positions.reshape(-1).astype(jnp.float32)[:, None] * inverse[None, :]
    return (jnp.cos(phase)[:, None, :], jnp.sin(phase)[:, None, :])


def shift(value, axis, step):
    n = lax.axis_size(axis)
    return lax.ppermute(value, axis, [(j, (j + step) % n) for j in range(n)])


def gather_axis(blocks, axis):
    n = lax.axis_size(axis)
    if n == 1:
        return blocks[None]
    if n == 2:
        return jnp.stack([blocks, shift(blocks, axis, 1)])
    assert n == 4
    from_prev = shift(blocks, axis, 1)
    from_next = shift(blocks, axis, -1)
    half = blocks.shape[-1] // 2
    far_a = shift(from_next[..., :half], axis, -1)
    far_b = shift(from_prev[..., half:], axis, 1)
    far = jnp.concatenate([far_a, far_b], axis=-1)
    return jnp.stack([blocks, from_next, far, from_prev])


def exchange_slices(local_rows):
    yhi = lax.axis_index("yhi")
    core = lax.axis_index("core")
    own = yhi * 2 + core
    pick = lambda t: lax.dynamic_index_in_dim(local_rows, t, axis=1, keepdims=False)
    mine = pick(own)
    from_core = shift(pick(yhi * 2 + (1 - core)), "core", 1)
    from_yhi = shift(pick((1 - yhi) * 2 + core), "yhi", 1)
    diag = 3 - own
    from_diag = lax.ppermute(
        pick(diag), ("yhi", "core"), [(j, 3 - j) for j in range(4)]
    )
    parts = []
    for p in range(4):
        k = p ^ own
        parts.append(
            jnp.where(k == 0, mine, jnp.where(k == 1, from_core, jnp.where(k == 2, from_yhi, from_diag)))
        )
    return jnp.concatenate(parts, axis=0)


def gather_first(block):
    paired = gather_axis(block, "ylo")
    half = block.shape[0] // 2
    return gather_axis(paired[:, :half], "x"), gather_axis(paired[:, half:], "z")


def gather_second(first):
    return gather_axis(first[0], "z"), gather_axis(first[1], "x")


def relative_columns(values, rows):
    tokens = values.shape[0]
    nx, nz, nl = (lax.axis_size(a) for a in ROW_AXES)
    ix, iz, il = (lax.axis_index(a) for a in ROW_AXES)
    grid = values.reshape(tokens, nx, nz, nl, rows)
    grid = jnp.roll(grid, -ix, axis=1)
    grid = jnp.roll(grid, -iz, axis=2)
    grid = jnp.roll(grid, -il, axis=3)
    half = rows // 2
    part_a = jnp.transpose(grid[..., :half], (0, 2, 1, 3, 4)).reshape(tokens, -1)
    part_b = grid[..., half:].reshape(tokens, -1)
    return part_a, part_b


def project(values, portions, rows):
    portion_a, portion_b = portions
    cols = portion_a.shape[-1]
    part_a, part_b = relative_columns(values, rows)
    first = jnp.dot(part_a, portion_a.reshape(-1, cols), preferred_element_type=jnp.float32)
    second = jnp.dot(part_b, portion_b.reshape(-1, cols), preferred_element_type=jnp.float32)
    return first + second


def local(
    hidden_in,
    norm_gain,
    query_weight,
    key_weight,
    value_weight,
    out_weight,
    query_bias,
    key_bias,
    value_bias,
    span_start,
    span_length,
):
    slices = lax.axis_size(COL_AXES)
    token_rows = hidden_in.shape[0]
    local_spans = span_start.shape[0]
    span_size = token_rows // local_spans
    query_cols = query_weight.shape[1] // slices
    key_cols = key_weight.shape[1] // slices
    learner_rows = query_weight.shape[0]
    block_rows = slices * learner_rows
    joined = jnp.concatenate(
        [
            query_weight.reshape(learner_rows, slices, query_cols),
            key_weight.reshape(learner_rows, slices, key_cols),
            value_weight.reshape(learner_rows, slices, key_cols),
        ],
        axis=2,
    )
    joined_block = exchange_slices(joined)
    qkv_portions = gather_second(gather_first(joined_block))
    qkv_portions, out_weight = lax.optimization_barrier((qkv_portions, out_weight))
    out_rows_local = out_weight.shape[0]
    out_cols = out_weight.shape[1] // slices
    out_block = exchange_slices(out_weight.reshape(out_rows_local, slices, out_cols))
    out_first = gather_first(out_block)
    gathered = lax.all_gather(hidden_in, COL_AXES, axis=1, tiled=True)
    source = gathered.astype(jnp.float32)
    inverse_rms = lax.rsqrt(jnp.mean(source * source, axis=-1, keepdims=True) + epsilon)
    normed = (source * inverse_rms * norm_gain.astype(jnp.float32)).astype(jnp.bfloat16)
    projected = project(normed, qkv_portions, block_rows)
    projected, out_first = lax.optimization_barrier((projected, out_first))
    out_portions = gather_second(out_first)
    query = projected[:, :query_cols] + query_bias.astype(jnp.float32)
    keys = projected[:, query_cols : query_cols + key_cols] + key_bias.astype(jnp.float32)
    values = projected[:, query_cols + key_cols :] + value_bias.astype(jnp.float32)
    local_heads = query_cols // HEAD
    local_kv = key_cols // HEAD
    groups = HEADS // KV_HEADS
    cosine, sine = angles(span_start, span_size)
    query = rotate(query.reshape(token_rows, local_heads, HEAD), cosine, sine).astype(jnp.bfloat16)
    keys = rotate(keys.reshape(token_rows, local_kv, HEAD), cosine, sine)
    live = (jnp.arange(span_size, dtype=jnp.int32)[None, :] < span_length[:, None]).reshape(
        token_rows, 1, 1
    )
    key_cache = jnp.where(live, keys, 0.0).astype(jnp.bfloat16)
    value_cache = jnp.where(live, values.reshape(token_rows, local_kv, HEAD), 0.0).astype(
        jnp.bfloat16
    )
    query_blocks = query.reshape(local_spans, span_size, local_kv, groups, HEAD)
    key_blocks = key_cache.reshape(local_spans, span_size, local_kv, HEAD)
    value_blocks = value_cache.reshape(local_spans, span_size, local_kv, HEAD)
    scores = jnp.einsum(
        "sqkgd,stkd->skgqt", query_blocks, key_blocks, preferred_element_type=jnp.float32
    ) * HEAD ** (-0.5)
    rows = jnp.arange(span_size, dtype=jnp.int32)[:, None]
    columns = jnp.arange(span_size, dtype=jnp.int32)[None, :]
    allowed = (columns <= rows)[None] & (columns[None] < span_length[:, None, None])
    scores = jnp.where(allowed[:, None, None], scores, -1e30)
    highest = jnp.max(scores, axis=-1, keepdims=True)
    raised = jnp.exp(scores - highest)
    probs = (raised / jnp.sum(raised, axis=-1, keepdims=True)).astype(jnp.bfloat16)
    mixed = jnp.einsum("skgqt,stkd->sqkgd", probs, value_blocks, preferred_element_type=jnp.float32)
    attended = mixed.reshape(token_rows, local_heads * HEAD).astype(jnp.bfloat16)
    attended, out_portions = lax.optimization_barrier((attended, out_portions))
    all_heads = lax.all_gather(attended, COL_AXES, axis=1, tiled=True)
    combined = project(all_heads, out_portions, block_rows)
    attention_out = combined.astype(jnp.bfloat16)
    return (
        attention_out,
        key_cache.reshape(token_rows, local_kv * HEAD),
        value_cache.reshape(token_rows, local_kv * HEAD),
    )


def physical_mesh(mesh):
    members = mesh.shape["fsdp"]
    slices = mesh.shape["tensor"]
    shape = (4, members // 8, 2, slices // 2, 2)
    return Mesh(np.asarray(mesh.devices).reshape(shape), ROW_AXES + COL_AXES)


def solution(mesh):
    fine = physical_mesh(mesh)
    rows = ROW_AXES
    both = ROW_AXES + COL_AXES
    placed = (
        P(rows, COL_AXES),
        P(),
        P(both, None),
        P(both, None),
        P(both, None),
        P(both, None),
        P(COL_AXES),
        P(COL_AXES),
        P(COL_AXES),
        P(rows),
        P(rows),
    )
    return jax.shard_map(
        local,
        mesh=fine,
        in_specs=placed,
        out_specs=(P(rows, COL_AXES), P(rows, COL_AXES), P(rows, COL_AXES)),
        check_vma=False,
    )
```

```python
import jax
import jax.numpy as jnp
import numpy as np
from jax import lax
from jax.sharding import Mesh
from jax.sharding import PartitionSpec as P

HEADS = 40
KV_HEADS = 8
HEAD = 128


rope_base = 1000000.0
epsilon = 1e-06

ROW_AXES = ("x", "z", "ylo")
COL_AXES = ("yhi", "core")


def rotate(entries, cosine, sine):
    half = entries.shape[-1] // 2
    first = entries[..., :half]
    second = entries[..., half:]
    return jnp.concatenate(
        [first * cosine - second * sine, second * cosine + first * sine], axis=-1
    )


def angles(span_start, span_size):
    positions = span_start[:, None] + jnp.arange(span_size, dtype=jnp.int32)[None, :]
    inverse = 1.0 / rope_base ** (jnp.arange(0, HEAD, 2, dtype=jnp.float32) / HEAD)
    phase = positions.reshape(-1).astype(jnp.float32)[:, None] * inverse[None, :]
    return (jnp.cos(phase)[:, None, :], jnp.sin(phase)[:, None, :])


def shift(value, axis, step):
    n = lax.axis_size(axis)
    return lax.ppermute(value, axis, [(j, (j + step) % n) for j in range(n)])


def gather_axis(blocks, axis):
    n = lax.axis_size(axis)
    if n == 1:
        return blocks[None]
    if n == 2:
        return jnp.stack([blocks, shift(blocks, axis, 1)])
    assert n == 4
    from_prev = shift(blocks, axis, 1)
    from_next = shift(blocks, axis, -1)
    half = blocks.shape[-1] // 2
    far_a = shift(from_next[..., :half], axis, -1)
    far_b = shift(from_prev[..., half:], axis, 1)
    far = jnp.concatenate([far_a, far_b], axis=-1)
    return jnp.stack([blocks, from_next, far, from_prev])


def exchange_slices(local_rows):
    yhi = lax.axis_index("yhi")
    core = lax.axis_index("core")
    own = yhi * 2 + core
    pick = lambda t: lax.dynamic_index_in_dim(local_rows, t, axis=1, keepdims=False)
    mine = pick(own)
    from_core = shift(pick(yhi * 2 + (1 - core)), "core", 1)
    from_yhi = shift(pick((1 - yhi) * 2 + core), "yhi", 1)
    diag = 3 - own
    from_diag = lax.ppermute(
        pick(diag), ("yhi", "core"), [(j, 3 - j) for j in range(4)]
    )
    parts = []
    for p in range(4):
        k = p ^ own
        parts.append(
            jnp.where(k == 0, mine, jnp.where(k == 1, from_core, jnp.where(k == 2, from_yhi, from_diag)))
        )
    return jnp.concatenate(parts, axis=0)


def gather_first(block):
    paired = gather_axis(block, "ylo")
    half = block.shape[0] // 2
    return gather_axis(paired[:, :half], "x"), gather_axis(paired[:, half:], "z")


def gather_second(first):
    return gather_axis(first[0], "z"), gather_axis(first[1], "x")


def relative_columns(values, rows):
    tokens = values.shape[0]
    nx, nz, nl = (lax.axis_size(a) for a in ROW_AXES)
    ix, iz, il = (lax.axis_index(a) for a in ROW_AXES)
    grid = values.reshape(tokens, nx, nz, nl, rows)
    grid = jnp.roll(grid, -ix, axis=1)
    grid = jnp.roll(grid, -iz, axis=2)
    grid = jnp.roll(grid, -il, axis=3)
    half = rows // 2
    part_a = jnp.transpose(grid[..., :half], (0, 2, 1, 3, 4)).reshape(tokens, -1)
    part_b = grid[..., half:].reshape(tokens, -1)
    return part_a, part_b


def project(values, portions, rows):
    portion_a, portion_b = portions
    cols = portion_a.shape[-1]
    part_a, part_b = relative_columns(values, rows)
    first = jnp.dot(part_a, portion_a.reshape(-1, cols), preferred_element_type=jnp.float32)
    second = jnp.dot(part_b, portion_b.reshape(-1, cols), preferred_element_type=jnp.float32)
    return first + second


def layer(
    hidden_in,
    norm_gain,
    query_weight,
    key_weight,
    value_weight,
    out_weight,
    query_bias,
    key_bias,
    value_bias,
    span_start,
    span_length,
):
    slices = lax.axis_size(COL_AXES)
    token_rows = hidden_in.shape[0]
    local_spans = span_start.shape[0]
    span_size = token_rows // local_spans
    query_cols = query_weight.shape[1] // slices
    key_cols = key_weight.shape[1] // slices
    learner_rows = query_weight.shape[0]
    block_rows = slices * learner_rows
    joined = jnp.concatenate(
        [
            query_weight.reshape(learner_rows, slices, query_cols),
            key_weight.reshape(learner_rows, slices, key_cols),
            value_weight.reshape(learner_rows, slices, key_cols),
        ],
        axis=2,
    )
    joined_block = exchange_slices(joined)
    qkv_portions = gather_second(gather_first(joined_block))
    qkv_portions, out_weight = lax.optimization_barrier((qkv_portions, out_weight))
    out_rows_local = out_weight.shape[0]
    out_cols = out_weight.shape[1] // slices
    out_block = exchange_slices(out_weight.reshape(out_rows_local, slices, out_cols))
    out_first = gather_first(out_block)
    gathered = lax.all_gather(hidden_in, COL_AXES, axis=1, tiled=True)
    source = gathered.astype(jnp.float32)
    inverse_rms = lax.rsqrt(jnp.mean(source * source, axis=-1, keepdims=True) + epsilon)
    normed = (source * inverse_rms * norm_gain.astype(jnp.float32)).astype(jnp.bfloat16)
    projected = project(normed, qkv_portions, block_rows)
    out_portions = gather_second(out_first)
    query = projected[:, :query_cols] + query_bias.astype(jnp.float32)
    keys = projected[:, query_cols : query_cols + key_cols] + key_bias.astype(jnp.float32)
    values = projected[:, query_cols + key_cols :] + value_bias.astype(jnp.float32)
    local_heads = query_cols // HEAD
    local_kv = key_cols // HEAD
    groups = HEADS // KV_HEADS
    cosine, sine = angles(span_start, span_size)
    query = rotate(query.reshape(token_rows, local_heads, HEAD), cosine, sine).astype(jnp.bfloat16)
    keys = rotate(keys.reshape(token_rows, local_kv, HEAD), cosine, sine)
    live = (jnp.arange(span_size, dtype=jnp.int32)[None, :] < span_length[:, None]).reshape(
        token_rows, 1, 1
    )
    key_cache = jnp.where(live, keys, 0.0).astype(jnp.bfloat16)
    value_cache = jnp.where(live, values.reshape(token_rows, local_kv, HEAD), 0.0).astype(
        jnp.bfloat16
    )
    query_blocks = query.reshape(local_spans, span_size, local_kv, groups, HEAD)
    key_blocks = key_cache.reshape(local_spans, span_size, local_kv, HEAD)
    value_blocks = value_cache.reshape(local_spans, span_size, local_kv, HEAD)
    scores = jnp.einsum(
        "sqkgd,stkd->skgqt", query_blocks, key_blocks, preferred_element_type=jnp.float32
    ) * HEAD ** (-0.5)
    rows = jnp.arange(span_size, dtype=jnp.int32)[:, None]
    columns = jnp.arange(span_size, dtype=jnp.int32)[None, :]
    allowed = (columns <= rows)[None] & (columns[None] < span_length[:, None, None])
    scores = jnp.where(allowed[:, None, None], scores, -1e30)
    highest = jnp.max(scores, axis=-1, keepdims=True)
    raised = jnp.exp(scores - highest)
    probs = (raised / jnp.sum(raised, axis=-1, keepdims=True)).astype(jnp.bfloat16)
    mixed = jnp.einsum("skgqt,stkd->sqkgd", probs, value_blocks, preferred_element_type=jnp.float32)
    attended = mixed.reshape(token_rows, local_heads * HEAD).astype(jnp.bfloat16)
    all_heads = lax.all_gather(attended, COL_AXES, axis=1, tiled=True)
    combined = project(all_heads, out_portions, block_rows)
    attention_out = combined.astype(jnp.bfloat16)
    return (
        attention_out,
        key_cache.reshape(token_rows, local_kv * HEAD),
        value_cache.reshape(token_rows, local_kv * HEAD),
    )


def physical_mesh(mesh):
    members = mesh.shape["fsdp"]
    slices = mesh.shape["tensor"]
    shape = (4, members // 8, 2, slices // 2, 2)
    return Mesh(np.asarray(mesh.devices).reshape(shape), ROW_AXES + COL_AXES)


def solution(mesh):
    fine = physical_mesh(mesh)
    rows = ROW_AXES
    both = ROW_AXES + COL_AXES
    placed = (
        P(rows, COL_AXES),
        P(),
        P(both, None),
        P(both, None),
        P(both, None),
        P(both, None),
        P(COL_AXES),
        P(COL_AXES),
        P(COL_AXES),
        P(rows),
        P(rows),
    )
    return jax.shard_map(
        layer,
        mesh=fine,
        in_specs=placed,
        out_specs=(P(rows, COL_AXES), P(rows, COL_AXES), P(rows, COL_AXES)),
        check_vma=False,
    )
```

```python
import jax
import jax.numpy as jnp
import numpy as np
from jax import lax
from jax.sharding import Mesh
from jax.sharding import PartitionSpec as P

HEADS = 40
KV_HEADS = 8
HEAD = 128


rope_base = 1000000.0
epsilon = 1e-06

ROW_AXES = ("x", "z", "ylo")
COL_AXES = ("yhi", "core")


def rotate(entries, cosine, sine):
    half = entries.shape[-1] // 2
    first = entries[..., :half]
    second = entries[..., half:]
    return jnp.concatenate(
        [first * cosine - second * sine, second * cosine + first * sine], axis=-1
    )


def angles(span_start, span_size):
    positions = span_start[:, None] + jnp.arange(span_size, dtype=jnp.int32)[None, :]
    inverse = 1.0 / rope_base ** (jnp.arange(0, HEAD, 2, dtype=jnp.float32) / HEAD)
    phase = positions.reshape(-1).astype(jnp.float32)[:, None] * inverse[None, :]
    return (jnp.cos(phase)[:, None, :], jnp.sin(phase)[:, None, :])


def shift(value, axis, step):
    n = lax.axis_size(axis)
    return lax.ppermute(value, axis, [(j, (j + step) % n) for j in range(n)])


def gather_axis(blocks, axis, stacked=True):
    n = lax.axis_size(axis)
    if n == 1:
        return blocks[None]
    if n == 2:
        return jnp.stack([blocks, shift(blocks, axis, 1)])
    assert n == 4
    from_prev = shift(blocks, axis, 1)
    from_next = shift(blocks, axis, -1)
    half = blocks.shape[-1] // 2
    far_a = shift(from_next[..., :half], axis, -1)
    far_b = shift(from_prev[..., half:], axis, 1)
    pieces = [blocks, from_next, (far_a, far_b), from_prev]
    return stack_pieces(pieces) if stacked else pieces


def stack_pieces(pieces):
    blocks, from_next, (far_a, far_b), from_prev = pieces
    far = jnp.concatenate([far_a, far_b], axis=-1)
    return jnp.stack([blocks, from_next, far, from_prev])


def exchange_slices(local_rows):
    yhi = lax.axis_index("yhi")
    core = lax.axis_index("core")
    own = yhi * 2 + core
    pick = lambda t: lax.dynamic_index_in_dim(local_rows, t, axis=1, keepdims=False)
    mine = pick(own)
    from_core = shift(pick(yhi * 2 + (1 - core)), "core", 1)
    from_yhi = shift(pick((1 - yhi) * 2 + core), "yhi", 1)
    diag = 3 - own
    from_diag = lax.ppermute(
        pick(diag), ("yhi", "core"), [(j, 3 - j) for j in range(4)]
    )
    parts = []
    for p in range(4):
        k = p ^ own
        parts.append(
            jnp.where(k == 0, mine, jnp.where(k == 1, from_core, jnp.where(k == 2, from_yhi, from_diag)))
        )
    return jnp.concatenate(parts, axis=0)


def gather_pair(block):
    return gather_axis(block, "ylo")


def gather_first(paired):
    half = paired.shape[1] // 2
    return gather_axis(paired[:, :half], "x"), gather_axis(paired[:, half:], "z")


def gather_second(first):
    return gather_axis(first[0], "z", False), gather_axis(first[1], "x", False)


def relative_columns(values, rows):
    tokens = values.shape[0]
    nx, nz, nl = (lax.axis_size(a) for a in ROW_AXES)
    ix, iz, il = (lax.axis_index(a) for a in ROW_AXES)
    grid = values.reshape(tokens, nx, nz, nl, rows)
    grid = jnp.roll(grid, -ix, axis=1)
    grid = jnp.roll(grid, -iz, axis=2)
    grid = jnp.roll(grid, -il, axis=3)
    half = rows // 2
    part_a = jnp.transpose(grid[..., :half], (0, 2, 1, 3, 4)).reshape(tokens, -1)
    part_b = grid[..., half:].reshape(tokens, -1)
    return part_a, part_b


def project(values, portions, rows):
    portion_a, portion_b = (stack_pieces(p) for p in portions)
    cols = portion_a.shape[-1]
    part_a, part_b = relative_columns(values, rows)
    first = jnp.dot(part_a, portion_a.reshape(-1, cols), preferred_element_type=jnp.float32)
    second = jnp.dot(part_b, portion_b.reshape(-1, cols), preferred_element_type=jnp.float32)
    return first + second


def layer(
    hidden_in,
    norm_gain,
    query_weight,
    key_weight,
    value_weight,
    out_weight,
    query_bias,
    key_bias,
    value_bias,
    span_start,
    span_length,
):
    slices = lax.axis_size(COL_AXES)
    token_rows = hidden_in.shape[0]
    local_spans = span_start.shape[0]
    span_size = token_rows // local_spans
    query_cols = query_weight.shape[1] // slices
    key_cols = key_weight.shape[1] // slices
    learner_rows = query_weight.shape[0]
    block_rows = slices * learner_rows
    joined = jnp.concatenate(
        [
            query_weight.reshape(learner_rows, slices, query_cols),
            key_weight.reshape(learner_rows, slices, key_cols),
            value_weight.reshape(learner_rows, slices, key_cols),
        ],
        axis=2,
    )
    qkv_paired = gather_pair(exchange_slices(joined))
    qkv_paired, out_weight = lax.optimization_barrier((qkv_paired, out_weight))
    qkv_portions = gather_second(gather_first(qkv_paired))
    out_rows_local = out_weight.shape[0]
    out_cols = out_weight.shape[1] // slices
    out_paired = gather_pair(exchange_slices(out_weight.reshape(out_rows_local, slices, out_cols)))
    qkv_portions, out_paired = lax.optimization_barrier((qkv_portions, out_paired))
    out_first = gather_first(out_paired)
    gathered = lax.all_gather(hidden_in, COL_AXES, axis=1, tiled=True)
    source = gathered.astype(jnp.float32)
    inverse_rms = lax.rsqrt(jnp.mean(source * source, axis=-1, keepdims=True) + epsilon)
    normed = (source * inverse_rms * norm_gain.astype(jnp.float32)).astype(jnp.bfloat16)
    projected = project(normed, qkv_portions, block_rows)
    out_portions = gather_second(out_first)
    query = projected[:, :query_cols] + query_bias.astype(jnp.float32)
    keys = projected[:, query_cols : query_cols + key_cols] + key_bias.astype(jnp.float32)
    values = projected[:, query_cols + key_cols :] + value_bias.astype(jnp.float32)
    local_heads = query_cols // HEAD
    local_kv = key_cols // HEAD
    groups = HEADS // KV_HEADS
    cosine, sine = angles(span_start, span_size)
    query = rotate(query.reshape(token_rows, local_heads, HEAD), cosine, sine).astype(jnp.bfloat16)
    keys = rotate(keys.reshape(token_rows, local_kv, HEAD), cosine, sine)
    live = (jnp.arange(span_size, dtype=jnp.int32)[None, :] < span_length[:, None]).reshape(
        token_rows, 1, 1
    )
    key_cache = jnp.where(live, keys, 0.0).astype(jnp.bfloat16)
    value_cache = jnp.where(live, values.reshape(token_rows, local_kv, HEAD), 0.0).astype(
        jnp.bfloat16
    )
    query_blocks = query.reshape(local_spans, span_size, local_kv, groups, HEAD)
    key_blocks = key_cache.reshape(local_spans, span_size, local_kv, HEAD)
    value_blocks = value_cache.reshape(local_spans, span_size, local_kv, HEAD)
    scores = jnp.einsum(
        "sqkgd,stkd->skgqt", query_blocks, key_blocks, preferred_element_type=jnp.float32
    ) * HEAD ** (-0.5)
    rows = jnp.arange(span_size, dtype=jnp.int32)[:, None]
    columns = jnp.arange(span_size, dtype=jnp.int32)[None, :]
    allowed = (columns <= rows)[None] & (columns[None] < span_length[:, None, None])
    scores = jnp.where(allowed[:, None, None], scores, -1e30)
    highest = jnp.max(scores, axis=-1, keepdims=True)
    raised = jnp.exp(scores - highest)
    probs = (raised / jnp.sum(raised, axis=-1, keepdims=True)).astype(jnp.bfloat16)
    mixed = jnp.einsum("skgqt,stkd->sqkgd", probs, value_blocks, preferred_element_type=jnp.float32)
    attended = mixed.reshape(token_rows, local_heads * HEAD).astype(jnp.bfloat16)
    all_heads = lax.all_gather(attended, COL_AXES, axis=1, tiled=True)
    combined = project(all_heads, out_portions, block_rows)
    attention_out = combined.astype(jnp.bfloat16)
    return (
        attention_out,
        key_cache.reshape(token_rows, local_kv * HEAD),
        value_cache.reshape(token_rows, local_kv * HEAD),
    )


def physical_mesh(mesh):
    members = mesh.shape["fsdp"]
    slices = mesh.shape["tensor"]
    shape = (4, members // 8, 2, slices // 2, 2)
    return Mesh(np.asarray(mesh.devices).reshape(shape), ROW_AXES + COL_AXES)


def solution(mesh):
    fine = physical_mesh(mesh)
    rows = ROW_AXES
    both = ROW_AXES + COL_AXES
    placed = (
        P(rows, COL_AXES),
        P(),
        P(both, None),
        P(both, None),
        P(both, None),
        P(both, None),
        P(COL_AXES),
        P(COL_AXES),
        P(COL_AXES),
        P(rows),
        P(rows),
    )
    return jax.shard_map(
        layer,
        mesh=fine,
        in_specs=placed,
        out_specs=(P(rows, COL_AXES), P(rows, COL_AXES), P(rows, COL_AXES)),
        check_vma=False,
    )
```

```python
import jax
import jax.numpy as jnp
import numpy as np
from jax import lax
from jax.sharding import Mesh
from jax.sharding import PartitionSpec as P

HEADS = 40
KV_HEADS = 8
HEAD = 128


rope_base = 1000000.0
epsilon = 1e-06

ROW_AXES = ("x", "z", "ylo")
COL_AXES = ("yhi", "core")


def rotate(entries, cosine, sine):
    half = entries.shape[-1] // 2
    first = entries[..., :half]
    second = entries[..., half:]
    return jnp.concatenate(
        [first * cosine - second * sine, second * cosine + first * sine], axis=-1
    )


def angles(span_start, span_size):
    positions = span_start[:, None] + jnp.arange(span_size, dtype=jnp.int32)[None, :]
    inverse = 1.0 / rope_base ** (jnp.arange(0, HEAD, 2, dtype=jnp.float32) / HEAD)
    phase = positions.reshape(-1).astype(jnp.float32)[:, None] * inverse[None, :]
    return (jnp.cos(phase)[:, None, :], jnp.sin(phase)[:, None, :])


def shift(value, axis, step):
    n = lax.axis_size(axis)
    return lax.ppermute(value, axis, [(j, (j + step) % n) for j in range(n)])


def gather_axis(blocks, axis, stacked=True):
    n = lax.axis_size(axis)
    if n == 1:
        return blocks[None]
    if n == 2:
        return jnp.stack([blocks, shift(blocks, axis, 1)])
    assert n == 4
    from_prev = shift(blocks, axis, 1)
    from_next = shift(blocks, axis, -1)
    half = blocks.shape[-1] // 2
    far_a = shift(from_next[..., :half], axis, -1)
    far_b = shift(from_prev[..., half:], axis, 1)
    pieces = [blocks, from_next, (far_a, far_b), from_prev]
    return stack_pieces(pieces) if stacked else pieces


def stack_pieces(pieces):
    blocks, from_next, (far_a, far_b), from_prev = pieces
    far = jnp.concatenate([far_a, far_b], axis=-1)
    return jnp.stack([blocks, from_next, far, from_prev])


def exchange_slices(local_rows):
    yhi = lax.axis_index("yhi")
    core = lax.axis_index("core")
    own = yhi * 2 + core
    pick = lambda t: lax.dynamic_index_in_dim(local_rows, t, axis=1, keepdims=False)
    mine = pick(own)
    from_core = shift(pick(yhi * 2 + (1 - core)), "core", 1)
    from_yhi = shift(pick((1 - yhi) * 2 + core), "yhi", 1)
    diag = 3 - own
    from_diag = lax.ppermute(
        pick(diag), ("yhi", "core"), [(j, 3 - j) for j in range(4)]
    )
    parts = []
    for p in range(4):
        k = p ^ own
        parts.append(
            jnp.where(k == 0, mine, jnp.where(k == 1, from_core, jnp.where(k == 2, from_yhi, from_diag)))
        )
    return jnp.concatenate(parts, axis=0)


def gather_pair(block):
    return gather_axis(block, "ylo")


def gather_first(paired):
    half = paired.shape[1] // 2
    return gather_axis(paired[:, :half], "x"), gather_axis(paired[:, half:], "z")


def gather_second(first):
    return gather_axis(first[0], "z", False), gather_axis(first[1], "x", False)


def relative_columns(values, rows):
    tokens = values.shape[0]
    nx, nz, nl = (lax.axis_size(a) for a in ROW_AXES)
    ix, iz, il = (lax.axis_index(a) for a in ROW_AXES)
    grid = values.reshape(tokens, nx, nz, nl, rows)
    grid = jnp.roll(grid, -ix, axis=1)
    grid = jnp.roll(grid, -iz, axis=2)
    grid = jnp.roll(grid, -il, axis=3)
    half = rows // 2
    part_a = jnp.transpose(grid[..., :half], (0, 2, 1, 3, 4)).reshape(tokens, -1)
    part_b = grid[..., half:].reshape(tokens, -1)
    return part_a, part_b


def project(parts, portions):
    portion_a, portion_b = (stack_pieces(p) for p in portions)
    cols = portion_a.shape[-1]
    part_a, part_b = parts
    first = jnp.dot(part_a, portion_a.reshape(-1, cols), preferred_element_type=jnp.float32)
    second = jnp.dot(part_b, portion_b.reshape(-1, cols), preferred_element_type=jnp.float32)
    return first + second


def layer(
    hidden_in,
    norm_gain,
    query_weight,
    key_weight,
    value_weight,
    out_weight,
    query_bias,
    key_bias,
    value_bias,
    span_start,
    span_length,
):
    slices = lax.axis_size(COL_AXES)
    token_rows = hidden_in.shape[0]
    local_spans = span_start.shape[0]
    span_size = token_rows // local_spans
    query_cols = query_weight.shape[1] // slices
    key_cols = key_weight.shape[1] // slices
    learner_rows = query_weight.shape[0]
    block_rows = slices * learner_rows
    joined = jnp.concatenate(
        [
            query_weight.reshape(learner_rows, slices, query_cols),
            key_weight.reshape(learner_rows, slices, key_cols),
            value_weight.reshape(learner_rows, slices, key_cols),
        ],
        axis=2,
    )
    qkv_paired = gather_pair(exchange_slices(joined))
    qkv_paired, out_weight = lax.optimization_barrier((qkv_paired, out_weight))
    qkv_portions = gather_second(gather_first(qkv_paired))
    out_rows_local = out_weight.shape[0]
    out_cols = out_weight.shape[1] // slices
    out_paired = gather_pair(exchange_slices(out_weight.reshape(out_rows_local, slices, out_cols)))
    qkv_portions, out_paired = lax.optimization_barrier((qkv_portions, out_paired))
    out_first = gather_first(out_paired)
    gathered = lax.all_gather(hidden_in, COL_AXES, axis=1, tiled=True)
    source = gathered.astype(jnp.float32)
    inverse_rms = lax.rsqrt(jnp.mean(source * source, axis=-1, keepdims=True) + epsilon)
    normed = (source * inverse_rms * norm_gain.astype(jnp.float32)).astype(jnp.bfloat16)
    normed_parts = relative_columns(normed, block_rows)
    projected = project(normed_parts, qkv_portions)
    out_portions = gather_second(out_first)
    query = projected[:, :query_cols] + query_bias.astype(jnp.float32)
    keys = projected[:, query_cols : query_cols + key_cols] + key_bias.astype(jnp.float32)
    values = projected[:, query_cols + key_cols :] + value_bias.astype(jnp.float32)
    local_heads = query_cols // HEAD
    local_kv = key_cols // HEAD
    groups = HEADS // KV_HEADS
    cosine, sine = angles(span_start, span_size)
    query = rotate(query.reshape(token_rows, local_heads, HEAD), cosine, sine).astype(jnp.bfloat16)
    keys = rotate(keys.reshape(token_rows, local_kv, HEAD), cosine, sine)
    live = (jnp.arange(span_size, dtype=jnp.int32)[None, :] < span_length[:, None]).reshape(
        token_rows, 1, 1
    )
    key_cache = jnp.where(live, keys, 0.0).astype(jnp.bfloat16)
    value_cache = jnp.where(live, values.reshape(token_rows, local_kv, HEAD), 0.0).astype(
        jnp.bfloat16
    )
    query_blocks = query.reshape(local_spans, span_size, local_kv, groups, HEAD)
    key_blocks = key_cache.reshape(local_spans, span_size, local_kv, HEAD)
    value_blocks = value_cache.reshape(local_spans, span_size, local_kv, HEAD)
    scores = jnp.einsum(
        "sqkgd,stkd->skgqt", query_blocks, key_blocks, preferred_element_type=jnp.float32
    ) * HEAD ** (-0.5)
    rows = jnp.arange(span_size, dtype=jnp.int32)[:, None]
    columns = jnp.arange(span_size, dtype=jnp.int32)[None, :]
    allowed = (columns <= rows)[None] & (columns[None] < span_length[:, None, None])
    scores = jnp.where(allowed[:, None, None], scores, -1e30)
    highest = jnp.max(scores, axis=-1, keepdims=True)
    raised = jnp.exp(scores - highest)
    probs = (raised / jnp.sum(raised, axis=-1, keepdims=True)).astype(jnp.bfloat16)
    mixed = jnp.einsum("skgqt,stkd->sqkgd", probs, value_blocks, preferred_element_type=jnp.float32)
    attended = mixed.reshape(token_rows, local_heads * HEAD).astype(jnp.bfloat16)
    all_heads = lax.all_gather(attended, COL_AXES, axis=1, tiled=True)
    combined = project(relative_columns(all_heads, block_rows), out_portions)
    attention_out = combined.astype(jnp.bfloat16)
    return (
        attention_out,
        key_cache.reshape(token_rows, local_kv * HEAD),
        value_cache.reshape(token_rows, local_kv * HEAD),
    )


def physical_mesh(mesh):
    members = mesh.shape["fsdp"]
    slices = mesh.shape["tensor"]
    shape = (4, members // 8, 2, slices // 2, 2)
    return Mesh(np.asarray(mesh.devices).reshape(shape), ROW_AXES + COL_AXES)


def solution(mesh):
    fine = physical_mesh(mesh)
    rows = ROW_AXES
    both = ROW_AXES + COL_AXES
    placed = (
        P(rows, COL_AXES),
        P(),
        P(both, None),
        P(both, None),
        P(both, None),
        P(both, None),
        P(COL_AXES),
        P(COL_AXES),
        P(COL_AXES),
        P(rows),
        P(rows),
    )
    return jax.shard_map(
        layer,
        mesh=fine,
        in_specs=placed,
        out_specs=(P(rows, COL_AXES), P(rows, COL_AXES), P(rows, COL_AXES)),
        check_vma=False,
    )
```

```python
import jax
import jax.numpy as jnp
import numpy as np
from jax import lax
from jax.sharding import Mesh
from jax.sharding import PartitionSpec as P

HEADS = 40
KV_HEADS = 8
HEAD = 128


rope_base = 1000000.0
epsilon = 1e-06

ROW_AXES = ("x", "z", "ylo")
COL_AXES = ("yhi", "core")


def rotate(entries, cosine, sine):
    half = entries.shape[-1] // 2
    first = entries[..., :half]
    second = entries[..., half:]
    return jnp.concatenate(
        [first * cosine - second * sine, second * cosine + first * sine], axis=-1
    )


def angles(span_start, span_size):
    positions = span_start[:, None] + jnp.arange(span_size, dtype=jnp.int32)[None, :]
    inverse = 1.0 / rope_base ** (jnp.arange(0, HEAD, 2, dtype=jnp.float32) / HEAD)
    phase = positions.reshape(-1).astype(jnp.float32)[:, None] * inverse[None, :]
    return (jnp.cos(phase)[:, None, :], jnp.sin(phase)[:, None, :])


def shift(value, axis, step):
    n = lax.axis_size(axis)
    return lax.ppermute(value, axis, [(j, (j + step) % n) for j in range(n)])


def gather_axis(blocks, axis, stacked=True):
    n = lax.axis_size(axis)
    if n == 1:
        return blocks[None]
    if n == 2:
        return jnp.stack([blocks, shift(blocks, axis, 1)])
    assert n == 4
    from_prev = shift(blocks, axis, 1)
    from_next = shift(blocks, axis, -1)
    half = blocks.shape[-1] // 2
    far_a = shift(from_next[..., :half], axis, -1)
    far_b = shift(from_prev[..., half:], axis, 1)
    pieces = [blocks, from_next, (far_a, far_b), from_prev]
    return stack_pieces(pieces) if stacked else pieces


def stack_pieces(pieces):
    blocks, from_next, (far_a, far_b), from_prev = pieces
    far = jnp.concatenate([far_a, far_b], axis=-1)
    return jnp.stack([blocks, from_next, far, from_prev])


def exchange_slices(local_rows):
    yhi = lax.axis_index("yhi")
    core = lax.axis_index("core")
    own = yhi * 2 + core
    pick = lambda t: lax.dynamic_index_in_dim(local_rows, t, axis=1, keepdims=False)
    mine = pick(own)
    from_core = shift(pick(yhi * 2 + (1 - core)), "core", 1)
    from_yhi = shift(pick((1 - yhi) * 2 + core), "yhi", 1)
    diag = 3 - own
    from_diag = lax.ppermute(
        pick(diag), ("yhi", "core"), [(j, 3 - j) for j in range(4)]
    )
    parts = []
    for p in range(4):
        k = p ^ own
        parts.append(
            jnp.where(k == 0, mine, jnp.where(k == 1, from_core, jnp.where(k == 2, from_yhi, from_diag)))
        )
    return jnp.concatenate(parts, axis=0)


def gather_heads(attended):
    yhi = lax.axis_index("yhi")
    core = lax.axis_index("core")
    across = shift(attended, "yhi", 1)
    pair = jnp.stack([jnp.where(yhi == 0, attended, across), jnp.where(yhi == 0, across, attended)])
    other = shift(pair, "core", 1)
    quad = jnp.stack([jnp.where(core == 0, pair, other), jnp.where(core == 0, other, pair)], axis=1)
    tokens = attended.shape[0]
    return jnp.transpose(quad, (2, 0, 1, 3)).reshape(tokens, -1)


def gather_pair(block):
    return gather_axis(block, "ylo")


def gather_first(paired):
    half = paired.shape[1] // 2
    return gather_axis(paired[:, :half], "x"), gather_axis(paired[:, half:], "z")


def gather_second(first):
    return gather_axis(first[0], "z", False), gather_axis(first[1], "x", False)


def relative_columns(values, rows):
    tokens = values.shape[0]
    nx, nz, nl = (lax.axis_size(a) for a in ROW_AXES)
    ix, iz, il = (lax.axis_index(a) for a in ROW_AXES)
    grid = values.reshape(tokens, nx, nz, nl, rows)
    grid = jnp.roll(grid, -ix, axis=1)
    grid = jnp.roll(grid, -iz, axis=2)
    grid = jnp.roll(grid, -il, axis=3)
    half = rows // 2
    part_a = jnp.transpose(grid[..., :half], (0, 2, 1, 3, 4)).reshape(tokens, -1)
    part_b = grid[..., half:].reshape(tokens, -1)
    return part_a, part_b


def project(parts, portions):
    portion_a, portion_b = (stack_pieces(p) for p in portions)
    cols = portion_a.shape[-1]
    part_a, part_b = parts
    first = jnp.dot(part_a, portion_a.reshape(-1, cols), preferred_element_type=jnp.float32)
    second = jnp.dot(part_b, portion_b.reshape(-1, cols), preferred_element_type=jnp.float32)
    return first + second


def layer(
    hidden_in,
    norm_gain,
    query_weight,
    key_weight,
    value_weight,
    out_weight,
    query_bias,
    key_bias,
    value_bias,
    span_start,
    span_length,
):
    slices = lax.axis_size(COL_AXES)
    token_rows = hidden_in.shape[0]
    local_spans = span_start.shape[0]
    span_size = token_rows // local_spans
    query_cols = query_weight.shape[1] // slices
    key_cols = key_weight.shape[1] // slices
    learner_rows = query_weight.shape[0]
    block_rows = slices * learner_rows
    joined = jnp.concatenate(
        [
            query_weight.reshape(learner_rows, slices, query_cols),
            key_weight.reshape(learner_rows, slices, key_cols),
            value_weight.reshape(learner_rows, slices, key_cols),
        ],
        axis=2,
    )
    qkv_paired = gather_pair(exchange_slices(joined))
    qkv_paired, out_weight = lax.optimization_barrier((qkv_paired, out_weight))
    qkv_portions = gather_second(gather_first(qkv_paired))
    out_rows_local = out_weight.shape[0]
    out_cols = out_weight.shape[1] // slices
    out_paired = gather_pair(exchange_slices(out_weight.reshape(out_rows_local, slices, out_cols)))
    qkv_portions, out_paired = lax.optimization_barrier((qkv_portions, out_paired))
    out_first = gather_first(out_paired)
    gathered = lax.all_gather(hidden_in, COL_AXES, axis=1, tiled=True)
    source = gathered.astype(jnp.float32)
    inverse_rms = lax.rsqrt(jnp.mean(source * source, axis=-1, keepdims=True) + epsilon)
    normed = (source * inverse_rms * norm_gain.astype(jnp.float32)).astype(jnp.bfloat16)
    normed_parts = relative_columns(normed, block_rows)
    projected = project(normed_parts, qkv_portions)
    out_portions = gather_second(out_first)
    query = projected[:, :query_cols] + query_bias.astype(jnp.float32)
    keys = projected[:, query_cols : query_cols + key_cols] + key_bias.astype(jnp.float32)
    values = projected[:, query_cols + key_cols :] + value_bias.astype(jnp.float32)
    local_heads = query_cols // HEAD
    local_kv = key_cols // HEAD
    groups = HEADS // KV_HEADS
    cosine, sine = angles(span_start, span_size)
    query = rotate(query.reshape(token_rows, local_heads, HEAD), cosine, sine).astype(jnp.bfloat16)
    keys = rotate(keys.reshape(token_rows, local_kv, HEAD), cosine, sine)
    live = (jnp.arange(span_size, dtype=jnp.int32)[None, :] < span_length[:, None]).reshape(
        token_rows, 1, 1
    )
    key_cache = jnp.where(live, keys, 0.0).astype(jnp.bfloat16)
    value_cache = jnp.where(live, values.reshape(token_rows, local_kv, HEAD), 0.0).astype(
        jnp.bfloat16
    )
    query_blocks = query.reshape(local_spans, span_size, local_kv, groups, HEAD)
    key_blocks = key_cache.reshape(local_spans, span_size, local_kv, HEAD)
    value_blocks = value_cache.reshape(local_spans, span_size, local_kv, HEAD)
    rows = jnp.arange(span_size, dtype=jnp.int32)[:, None]
    columns = jnp.arange(span_size, dtype=jnp.int32)[None, :]
    pieces = []
    for s in range(local_spans):
        scores = jnp.einsum(
            "qkgd,tkd->kgqt", query_blocks[s], key_blocks[s], preferred_element_type=jnp.float32
        ) * HEAD ** (-0.5)
        allowed = (columns <= rows) & (columns < span_length[s])
        scores = jnp.where(allowed, scores, -1e30)
        highest = jnp.max(scores, axis=-1, keepdims=True)
        raised = jnp.exp(scores - highest)
        probs = (raised / jnp.sum(raised, axis=-1, keepdims=True)).astype(jnp.bfloat16)
        mixed = jnp.einsum(
            "kgqt,tkd->qkgd", probs, value_blocks[s], preferred_element_type=jnp.float32
        )
        attended = mixed.reshape(span_size, local_heads * HEAD).astype(jnp.bfloat16)
        all_heads = gather_heads(attended)
        pieces.append(project(relative_columns(all_heads, block_rows), out_portions))
    combined = jnp.concatenate(pieces, axis=0)
    attention_out = combined.astype(jnp.bfloat16)
    return (
        attention_out,
        key_cache.reshape(token_rows, local_kv * HEAD),
        value_cache.reshape(token_rows, local_kv * HEAD),
    )


def physical_mesh(mesh):
    members = mesh.shape["fsdp"]
    slices = mesh.shape["tensor"]
    shape = (4, members // 8, 2, slices // 2, 2)
    return Mesh(np.asarray(mesh.devices).reshape(shape), ROW_AXES + COL_AXES)


def solution(mesh):
    fine = physical_mesh(mesh)
    rows = ROW_AXES
    both = ROW_AXES + COL_AXES
    placed = (
        P(rows, COL_AXES),
        P(),
        P(both, None),
        P(both, None),
        P(both, None),
        P(both, None),
        P(COL_AXES),
        P(COL_AXES),
        P(COL_AXES),
        P(rows),
        P(rows),
    )
    return jax.shard_map(
        layer,
        mesh=fine,
        in_specs=placed,
        out_specs=(P(rows, COL_AXES), P(rows, COL_AXES), P(rows, COL_AXES)),
        check_vma=False,
    )
```

```python
import functools

import jax
import jax.numpy as jnp
import numpy as np
from jax import lax
from jax.experimental import pallas as pl
from jax.experimental.pallas import tpu as pltpu
from jax.sharding import Mesh
from jax.sharding import PartitionSpec as P

HEADS = 40
KV_HEADS = 8
HEAD = 128


rope_base = 1000000.0
epsilon = 1e-06

ROW_AXES = ("x", "z", "ylo")
COL_AXES = ("yhi", "core")


def rotate(entries, cosine, sine):
    half = entries.shape[-1] // 2
    first = entries[..., :half]
    second = entries[..., half:]
    return jnp.concatenate(
        [first * cosine - second * sine, second * cosine + first * sine], axis=-1
    )


def angles(span_start, span_size):
    positions = span_start[:, None] + jnp.arange(span_size, dtype=jnp.int32)[None, :]
    inverse = 1.0 / rope_base ** (jnp.arange(0, HEAD, 2, dtype=jnp.float32) / HEAD)
    phase = positions.reshape(-1).astype(jnp.float32)[:, None] * inverse[None, :]
    return (jnp.cos(phase)[:, None, :], jnp.sin(phase)[:, None, :])


def attention_kernel(lengths_ref, q_ref, k_ref, v_ref, o_ref, *, groups, scale):
    s = pl.program_id(0)
    length = lengths_ref[s]
    span = q_ref.shape[0]
    rows = lax.broadcasted_iota(jnp.int32, (span, span), 0)
    cols = lax.broadcasted_iota(jnp.int32, (span, span), 1)
    allowed = (cols <= rows) & (cols < length)
    k = k_ref[...]
    v = v_ref[...]
    for j in range(groups):
        q = q_ref[:, j * HEAD:(j + 1) * HEAD]
        scores = lax.dot_general(
            q, k, (((1,), (1,)), ((), ())), preferred_element_type=jnp.float32
        ) * scale
        scores = jnp.where(allowed, scores, -1e30)
        highest = jnp.max(scores, axis=-1, keepdims=True)
        raised = jnp.exp(scores - highest)
        probs = (raised / jnp.sum(raised, axis=-1, keepdims=True)).astype(jnp.bfloat16)
        mixed = jnp.dot(probs, v, preferred_element_type=jnp.float32)
        o_ref[:, j * HEAD:(j + 1) * HEAD] = mixed.astype(o_ref.dtype)


def attention(query, key_cache, value_cache, span_length, span, groups, interpret=False):
    tokens, qcols = query.shape
    kv = key_cache.shape[1] // HEAD
    spans = tokens // span
    kernel = functools.partial(attention_kernel, groups=groups, scale=HEAD ** (-0.5))
    return pl.pallas_call(
        kernel,
        out_shape=jax.ShapeDtypeStruct((tokens, qcols), jnp.bfloat16),
        grid_spec=pltpu.PrefetchScalarGridSpec(
            num_scalar_prefetch=1,
            grid=(spans, kv),
            in_specs=[
                pl.BlockSpec((span, groups * HEAD), lambda s, g, lens: (s, g)),
                pl.BlockSpec((span, HEAD), lambda s, g, lens: (s, g)),
                pl.BlockSpec((span, HEAD), lambda s, g, lens: (s, g)),
            ],
            out_specs=pl.BlockSpec((span, groups * HEAD), lambda s, g, lens: (s, g)),
        ),
        interpret=interpret,
    )(span_length, query, key_cache, value_cache)


def shift(value, axis, step):
    n = lax.axis_size(axis)
    return lax.ppermute(value, axis, [(j, (j + step) % n) for j in range(n)])


def gather_axis(blocks, axis, stacked=True):
    n = lax.axis_size(axis)
    if n == 1:
        return blocks[None]
    if n == 2:
        return jnp.stack([blocks, shift(blocks, axis, 1)])
    assert n == 4
    from_prev = shift(blocks, axis, 1)
    from_next = shift(blocks, axis, -1)
    half = blocks.shape[-1] // 2
    far_a = shift(from_next[..., :half], axis, -1)
    far_b = shift(from_prev[..., half:], axis, 1)
    pieces = [blocks, from_next, (far_a, far_b), from_prev]
    return stack_pieces(pieces) if stacked else pieces


def stack_pieces(pieces, axis=0):
    blocks, from_next, (far_a, far_b), from_prev = pieces
    far = jnp.concatenate([far_a, far_b], axis=-1)
    return jnp.stack([blocks, from_next, far, from_prev], axis=axis)


def exchange_slices(local_rows):
    yhi = lax.axis_index("yhi")
    core = lax.axis_index("core")
    own = yhi * 2 + core
    pick = lambda t: lax.dynamic_index_in_dim(local_rows, t, axis=1, keepdims=False)
    mine = pick(own)
    from_core = shift(pick(yhi * 2 + (1 - core)), "core", 1)
    from_yhi = shift(pick((1 - yhi) * 2 + core), "yhi", 1)
    diag = 3 - own
    from_diag = lax.ppermute(
        pick(diag), ("yhi", "core"), [(j, 3 - j) for j in range(4)]
    )
    parts = []
    for p in range(4):
        k = p ^ own
        parts.append(
            jnp.where(k == 0, mine, jnp.where(k == 1, from_core, jnp.where(k == 2, from_yhi, from_diag)))
        )
    return jnp.concatenate(parts, axis=0)


def gather_heads(attended):
    yhi = lax.axis_index("yhi")
    core = lax.axis_index("core")
    across = shift(attended, "yhi", 1)
    pair = jnp.stack([jnp.where(yhi == 0, attended, across), jnp.where(yhi == 0, across, attended)])
    other = shift(pair, "core", 1)
    quad = jnp.stack([jnp.where(core == 0, pair, other), jnp.where(core == 0, other, pair)], axis=1)
    tokens = attended.shape[0]
    return jnp.transpose(quad, (2, 0, 1, 3)).reshape(tokens, -1)


def gather_pair(block):
    return gather_axis(block, "ylo")


def gather_first(paired):
    half = paired.shape[1] // 2
    return gather_axis(paired[:, :half], "x"), gather_axis(paired[:, half:], "z")


def gather_second(first):
    return gather_axis(first[0], "z", False), gather_axis(first[1], "x", False)


def relative_columns(values, rows):
    tokens = values.shape[0]
    nx, nz, nl = (lax.axis_size(a) for a in ROW_AXES)
    ix, iz, il = (lax.axis_index(a) for a in ROW_AXES)
    grid = values.reshape(tokens, nx, nz, nl, rows)
    grid = jnp.roll(grid, -ix, axis=1)
    grid = jnp.roll(grid, -iz, axis=2)
    grid = jnp.roll(grid, -il, axis=3)
    half = rows // 2
    part_a = grid[..., :half].reshape(tokens, -1)
    part_b = grid[..., half:].reshape(tokens, -1)
    return part_a, part_b


def project(parts, portions):
    portion_a = stack_pieces(portions[0], axis=1)
    portion_b = stack_pieces(portions[1])
    cols = portion_a.shape[-1]
    part_a, part_b = parts
    first = jnp.dot(part_a, portion_a.reshape(-1, cols), preferred_element_type=jnp.float32)
    second = jnp.dot(part_b, portion_b.reshape(-1, cols), preferred_element_type=jnp.float32)
    return first + second


def layer(
    hidden_in,
    norm_gain,
    query_weight,
    key_weight,
    value_weight,
    out_weight,
    query_bias,
    key_bias,
    value_bias,
    span_start,
    span_length,
):
    slices = lax.axis_size(COL_AXES)
    token_rows = hidden_in.shape[0]
    local_spans = span_start.shape[0]
    span_size = token_rows // local_spans
    query_cols = query_weight.shape[1] // slices
    key_cols = key_weight.shape[1] // slices
    learner_rows = query_weight.shape[0]
    block_rows = slices * learner_rows
    joined = jnp.concatenate(
        [
            query_weight.reshape(learner_rows, slices, query_cols),
            key_weight.reshape(learner_rows, slices, key_cols),
            value_weight.reshape(learner_rows, slices, key_cols),
        ],
        axis=2,
    )
    qkv_paired = gather_pair(exchange_slices(joined))
    qkv_paired, out_weight = lax.optimization_barrier((qkv_paired, out_weight))
    qkv_portions = gather_second(gather_first(qkv_paired))
    out_rows_local = out_weight.shape[0]
    out_cols = out_weight.shape[1] // slices
    out_paired = gather_pair(exchange_slices(out_weight.reshape(out_rows_local, slices, out_cols)))
    qkv_portions, out_paired = lax.optimization_barrier((qkv_portions, out_paired))
    out_first = gather_first(out_paired)
    gathered = lax.all_gather(hidden_in, COL_AXES, axis=1, tiled=True)
    source = gathered.astype(jnp.float32)
    inverse_rms = lax.rsqrt(jnp.mean(source * source, axis=-1, keepdims=True) + epsilon)
    normed = (source * inverse_rms * norm_gain.astype(jnp.float32)).astype(jnp.bfloat16)
    normed_parts = relative_columns(normed, block_rows)
    projected = project(normed_parts, qkv_portions)
    out_portions = gather_second(out_first)
    query = projected[:, :query_cols] + query_bias.astype(jnp.float32)
    keys = projected[:, query_cols : query_cols + key_cols] + key_bias.astype(jnp.float32)
    values = projected[:, query_cols + key_cols :] + value_bias.astype(jnp.float32)
    local_heads = query_cols // HEAD
    local_kv = key_cols // HEAD
    groups = HEADS // KV_HEADS
    cosine, sine = angles(span_start, span_size)
    query = rotate(query.reshape(token_rows, local_heads, HEAD), cosine, sine).astype(jnp.bfloat16)
    keys = rotate(keys.reshape(token_rows, local_kv, HEAD), cosine, sine)
    live = (jnp.arange(span_size, dtype=jnp.int32)[None, :] < span_length[:, None]).reshape(
        token_rows, 1, 1
    )
    key_cache = jnp.where(live, keys, 0.0).astype(jnp.bfloat16)
    value_cache = jnp.where(live, values.reshape(token_rows, local_kv, HEAD), 0.0).astype(
        jnp.bfloat16
    )
    attended = attention(
        query.reshape(token_rows, local_heads * HEAD),
        key_cache.reshape(token_rows, local_kv * HEAD),
        value_cache.reshape(token_rows, local_kv * HEAD),
        span_length,
        span_size,
        groups,
    )
    all_heads = gather_heads(attended)
    combined = project(relative_columns(all_heads, block_rows), out_portions)
    attention_out = combined.astype(jnp.bfloat16)
    return (
        attention_out,
        key_cache.reshape(token_rows, local_kv * HEAD),
        value_cache.reshape(token_rows, local_kv * HEAD),
    )


def physical_mesh(mesh):
    members = mesh.shape["fsdp"]
    slices = mesh.shape["tensor"]
    shape = (4, members // 8, 2, slices // 2, 2)
    return Mesh(np.asarray(mesh.devices).reshape(shape), ROW_AXES + COL_AXES)


def solution(mesh):
    fine = physical_mesh(mesh)
    rows = ROW_AXES
    both = ROW_AXES + COL_AXES
    placed = (
        P(rows, COL_AXES),
        P(),
        P(both, None),
        P(both, None),
        P(both, None),
        P(both, None),
        P(COL_AXES),
        P(COL_AXES),
        P(COL_AXES),
        P(rows),
        P(rows),
    )
    return jax.shard_map(
        layer,
        mesh=fine,
        in_specs=placed,
        out_specs=(P(rows, COL_AXES), P(rows, COL_AXES), P(rows, COL_AXES)),
        check_vma=False,
    )
```

```python
import functools

import jax
import jax.numpy as jnp
import numpy as np
from jax import lax
from jax.experimental import pallas as pl
from jax.experimental.pallas import tpu as pltpu
from jax.sharding import Mesh
from jax.sharding import PartitionSpec as P

HEADS = 40
KV_HEADS = 8
HEAD = 128


rope_base = 1000000.0
epsilon = 1e-06

ROW_AXES = ("x", "z", "ylo")
COL_AXES = ("yhi", "core")


def rotate(entries, cosine, sine):
    half = entries.shape[-1] // 2
    first = entries[..., :half]
    second = entries[..., half:]
    return jnp.concatenate(
        [first * cosine - second * sine, second * cosine + first * sine], axis=-1
    )


def angles(span_start, span_size):
    positions = span_start[:, None] + jnp.arange(span_size, dtype=jnp.int32)[None, :]
    inverse = 1.0 / rope_base ** (jnp.arange(0, HEAD, 2, dtype=jnp.float32) / HEAD)
    phase = positions.reshape(-1).astype(jnp.float32)[:, None] * inverse[None, :]
    return (jnp.cos(phase)[:, None, :], jnp.sin(phase)[:, None, :])


def attention_kernel(lengths_ref, q_ref, k_ref, v_ref, o_ref, *, groups, scale):
    s = pl.program_id(0)
    length = lengths_ref[s]
    span = q_ref.shape[0]
    rows = lax.broadcasted_iota(jnp.int32, (span, span), 0)
    cols = lax.broadcasted_iota(jnp.int32, (span, span), 1)
    allowed = (cols <= rows) & (cols < length)
    k = k_ref[...]
    v = v_ref[...]
    for j in range(groups):
        q = q_ref[:, j * HEAD:(j + 1) * HEAD]
        scores = lax.dot_general(
            q, k, (((1,), (1,)), ((), ())), preferred_element_type=jnp.float32
        ) * scale
        scores = jnp.where(allowed, scores, -1e30)
        highest = jnp.max(scores, axis=-1, keepdims=True)
        raised = jnp.exp(scores - highest)
        probs = (raised / jnp.sum(raised, axis=-1, keepdims=True)).astype(jnp.bfloat16)
        mixed = jnp.dot(probs, v, preferred_element_type=jnp.float32)
        o_ref[:, j * HEAD:(j + 1) * HEAD] = mixed.astype(o_ref.dtype)


def attention(query, key_cache, value_cache, span_length, span, groups, interpret=False):
    tokens, qcols = query.shape
    kv = key_cache.shape[1] // HEAD
    spans = tokens // span
    kernel = functools.partial(attention_kernel, groups=groups, scale=HEAD ** (-0.5))
    return pl.pallas_call(
        kernel,
        out_shape=jax.ShapeDtypeStruct((tokens, qcols), jnp.bfloat16),
        grid_spec=pltpu.PrefetchScalarGridSpec(
            num_scalar_prefetch=1,
            grid=(spans, kv),
            in_specs=[
                pl.BlockSpec((span, groups * HEAD), lambda s, g, lens: (s, g)),
                pl.BlockSpec((span, HEAD), lambda s, g, lens: (s, g)),
                pl.BlockSpec((span, HEAD), lambda s, g, lens: (s, g)),
            ],
            out_specs=pl.BlockSpec((span, groups * HEAD), lambda s, g, lens: (s, g)),
        ),
        interpret=interpret,
    )(span_length, query, key_cache, value_cache)


def shift(value, axis, step):
    n = lax.axis_size(axis)
    return lax.ppermute(value, axis, [(j, (j + step) % n) for j in range(n)])


def gather_axis(blocks, axis, stacked=True):
    n = lax.axis_size(axis)
    if n == 1:
        return blocks[None]
    if n == 2:
        return jnp.stack([blocks, shift(blocks, axis, 1)])
    assert n == 4
    from_prev = shift(blocks, axis, 1)
    from_next = shift(blocks, axis, -1)
    half = blocks.shape[-1] // 2
    far_a = shift(from_next[..., :half], axis, -1)
    far_b = shift(from_prev[..., half:], axis, 1)
    pieces = [blocks, from_next, (far_a, far_b), from_prev]
    return stack_pieces(pieces) if stacked else pieces


def stack_pieces(pieces):
    blocks, from_next, (far_a, far_b), from_prev = pieces
    far = jnp.concatenate([far_a, far_b], axis=-1)
    return jnp.stack([blocks, from_next, far, from_prev])


def exchange_slices(local_rows):
    yhi = lax.axis_index("yhi")
    core = lax.axis_index("core")
    own = yhi * 2 + core
    pick = lambda t: lax.dynamic_index_in_dim(local_rows, t, axis=1, keepdims=False)
    mine = pick(own)
    from_core = shift(pick(yhi * 2 + (1 - core)), "core", 1)
    from_yhi = shift(pick((1 - yhi) * 2 + core), "yhi", 1)
    diag = 3 - own
    from_diag = lax.ppermute(
        pick(diag), ("yhi", "core"), [(j, 3 - j) for j in range(4)]
    )
    parts = []
    for p in range(4):
        k = p ^ own
        parts.append(
            jnp.where(k == 0, mine, jnp.where(k == 1, from_core, jnp.where(k == 2, from_yhi, from_diag)))
        )
    return jnp.concatenate(parts, axis=0)


def gather_heads(attended):
    yhi = lax.axis_index("yhi")
    core = lax.axis_index("core")
    across = shift(attended, "yhi", 1)
    pair = jnp.stack([jnp.where(yhi == 0, attended, across), jnp.where(yhi == 0, across, attended)])
    other = shift(pair, "core", 1)
    quad = jnp.stack([jnp.where(core == 0, pair, other), jnp.where(core == 0, other, pair)], axis=1)
    tokens = attended.shape[0]
    return jnp.transpose(quad, (2, 0, 1, 3)).reshape(tokens, -1)


def gather_pair(block):
    return gather_axis(block, "ylo")


def gather_first(paired):
    half = paired.shape[1] // 2
    return gather_axis(paired[:, :half], "x"), gather_axis(paired[:, half:], "z")


def gather_second(first):
    return gather_axis(first[0], "z", False), gather_axis(first[1], "x", False)


def relative_columns(values, rows):
    tokens = values.shape[0]
    nx, nz, nl = (lax.axis_size(a) for a in ROW_AXES)
    ix, iz, il = (lax.axis_index(a) for a in ROW_AXES)
    grid = values.reshape(tokens, nx, nz, nl, rows)
    grid = jnp.roll(grid, -ix, axis=1)
    grid = jnp.roll(grid, -iz, axis=2)
    grid = jnp.roll(grid, -il, axis=3)
    half = rows // 2
    part_a = jnp.transpose(grid[..., :half], (0, 2, 1, 3, 4)).reshape(tokens, -1)
    part_b = grid[..., half:].reshape(tokens, -1)
    return part_a, part_b


def project(parts, portions):
    portion_a, portion_b = (stack_pieces(p) for p in portions)
    cols = portion_a.shape[-1]
    part_a, part_b = parts
    first = jnp.dot(part_a, portion_a.reshape(-1, cols), preferred_element_type=jnp.float32)
    second = jnp.dot(part_b, portion_b.reshape(-1, cols), preferred_element_type=jnp.float32)
    return first + second


def layer(
    hidden_in,
    norm_gain,
    query_weight,
    key_weight,
    value_weight,
    out_weight,
    query_bias,
    key_bias,
    value_bias,
    span_start,
    span_length,
):
    slices = lax.axis_size(COL_AXES)
    token_rows = hidden_in.shape[0]
    local_spans = span_start.shape[0]
    span_size = token_rows // local_spans
    query_cols = query_weight.shape[1] // slices
    key_cols = key_weight.shape[1] // slices
    learner_rows = query_weight.shape[0]
    block_rows = slices * learner_rows
    joined = jnp.concatenate(
        [
            query_weight.reshape(learner_rows, slices, query_cols),
            key_weight.reshape(learner_rows, slices, key_cols),
            value_weight.reshape(learner_rows, slices, key_cols),
        ],
        axis=2,
    )
    qkv_paired = gather_pair(exchange_slices(joined))
    qkv_paired, out_weight, hidden_in = lax.optimization_barrier((qkv_paired, out_weight, hidden_in))
    qkv_portions = gather_second(gather_first(qkv_paired))
    out_rows_local = out_weight.shape[0]
    out_cols = out_weight.shape[1] // slices
    out_paired = gather_pair(exchange_slices(out_weight.reshape(out_rows_local, slices, out_cols)))
    out_first = gather_first(out_paired)
    qkv_portions, out_first = lax.optimization_barrier((qkv_portions, out_first))
    gathered = lax.all_gather(hidden_in, COL_AXES, axis=1, tiled=True)
    source = gathered.astype(jnp.float32)
    inverse_rms = lax.rsqrt(jnp.mean(source * source, axis=-1, keepdims=True) + epsilon)
    normed = (source * inverse_rms * norm_gain.astype(jnp.float32)).astype(jnp.bfloat16)
    normed_parts = relative_columns(normed, block_rows)
    projected = project(normed_parts, qkv_portions)
    out_portions = gather_second(out_first)
    query = projected[:, :query_cols] + query_bias.astype(jnp.float32)
    keys = projected[:, query_cols : query_cols + key_cols] + key_bias.astype(jnp.float32)
    values = projected[:, query_cols + key_cols :] + value_bias.astype(jnp.float32)
    local_heads = query_cols // HEAD
    local_kv = key_cols // HEAD
    groups = HEADS // KV_HEADS
    cosine, sine = angles(span_start, span_size)
    query = rotate(query.reshape(token_rows, local_heads, HEAD), cosine, sine).astype(jnp.bfloat16)
    keys = rotate(keys.reshape(token_rows, local_kv, HEAD), cosine, sine)
    live = (jnp.arange(span_size, dtype=jnp.int32)[None, :] < span_length[:, None]).reshape(
        token_rows, 1, 1
    )
    key_cache = jnp.where(live, keys, 0.0).astype(jnp.bfloat16)
    value_cache = jnp.where(live, values.reshape(token_rows, local_kv, HEAD), 0.0).astype(
        jnp.bfloat16
    )
    attended = attention(
        query.reshape(token_rows, local_heads * HEAD),
        key_cache.reshape(token_rows, local_kv * HEAD),
        value_cache.reshape(token_rows, local_kv * HEAD),
        span_length,
        span_size,
        groups,
    )
    all_heads = gather_heads(attended)
    combined = project(relative_columns(all_heads, block_rows), out_portions)
    attention_out = combined.astype(jnp.bfloat16)
    return (
        attention_out,
        key_cache.reshape(token_rows, local_kv * HEAD),
        value_cache.reshape(token_rows, local_kv * HEAD),
    )


def physical_mesh(mesh):
    members = mesh.shape["fsdp"]
    slices = mesh.shape["tensor"]
    shape = (4, members // 8, 2, slices // 2, 2)
    return Mesh(np.asarray(mesh.devices).reshape(shape), ROW_AXES + COL_AXES)


def solution(mesh):
    fine = physical_mesh(mesh)
    rows = ROW_AXES
    both = ROW_AXES + COL_AXES
    placed = (
        P(rows, COL_AXES),
        P(),
        P(both, None),
        P(both, None),
        P(both, None),
        P(both, None),
        P(COL_AXES),
        P(COL_AXES),
        P(COL_AXES),
        P(rows),
        P(rows),
    )
    return jax.shard_map(
        layer,
        mesh=fine,
        in_specs=placed,
        out_specs=(P(rows, COL_AXES), P(rows, COL_AXES), P(rows, COL_AXES)),
        check_vma=False,
    )
```

```python
import functools

import jax
import jax.numpy as jnp
import numpy as np
from jax import lax
from jax.experimental import pallas as pl
from jax.experimental.pallas import tpu as pltpu
from jax.sharding import Mesh
from jax.sharding import PartitionSpec as P

HEADS = 40
KV_HEADS = 8
HEAD = 128


rope_base = 1000000.0
epsilon = 1e-06

ROW_AXES = ("x", "z", "ylo")
COL_AXES = ("yhi", "core")


def rotate(entries, cosine, sine):
    half = entries.shape[-1] // 2
    first = entries[..., :half]
    second = entries[..., half:]
    return jnp.concatenate(
        [first * cosine - second * sine, second * cosine + first * sine], axis=-1
    )


def angles(span_start, span_size):
    positions = span_start[:, None] + jnp.arange(span_size, dtype=jnp.int32)[None, :]
    inverse = 1.0 / rope_base ** (jnp.arange(0, HEAD, 2, dtype=jnp.float32) / HEAD)
    phase = positions.reshape(-1).astype(jnp.float32)[:, None] * inverse[None, :]
    return (jnp.cos(phase)[:, None, :], jnp.sin(phase)[:, None, :])


def attention_kernel(lengths_ref, q_ref, k_ref, v_ref, o_ref, *, groups, scale):
    s = pl.program_id(0)
    length = lengths_ref[s]
    span = q_ref.shape[0]
    rows = lax.broadcasted_iota(jnp.int32, (span, span), 0)
    cols = lax.broadcasted_iota(jnp.int32, (span, span), 1)
    allowed = (cols <= rows) & (cols < length)
    k = k_ref[...]
    v = v_ref[...]
    for j in range(groups):
        q = q_ref[:, j * HEAD:(j + 1) * HEAD]
        scores = lax.dot_general(
            q, k, (((1,), (1,)), ((), ())), preferred_element_type=jnp.float32
        ) * scale
        scores = jnp.where(allowed, scores, -1e30)
        highest = jnp.max(scores, axis=-1, keepdims=True)
        raised = jnp.exp(scores - highest)
        probs = (raised / jnp.sum(raised, axis=-1, keepdims=True)).astype(jnp.bfloat16)
        mixed = jnp.dot(probs, v, preferred_element_type=jnp.float32)
        o_ref[:, j * HEAD:(j + 1) * HEAD] = mixed.astype(o_ref.dtype)


def attention(query, key_cache, value_cache, span_length, span, groups, interpret=False):
    tokens, qcols = query.shape
    kv = key_cache.shape[1] // HEAD
    spans = tokens // span
    kernel = functools.partial(attention_kernel, groups=groups, scale=HEAD ** (-0.5))
    return pl.pallas_call(
        kernel,
        out_shape=jax.ShapeDtypeStruct((tokens, qcols), jnp.bfloat16),
        grid_spec=pltpu.PrefetchScalarGridSpec(
            num_scalar_prefetch=1,
            grid=(spans, kv),
            in_specs=[
                pl.BlockSpec((span, groups * HEAD), lambda s, g, lens: (s, g)),
                pl.BlockSpec((span, HEAD), lambda s, g, lens: (s, g)),
                pl.BlockSpec((span, HEAD), lambda s, g, lens: (s, g)),
            ],
            out_specs=pl.BlockSpec((span, groups * HEAD), lambda s, g, lens: (s, g)),
        ),
        interpret=interpret,
    )(span_length, query, key_cache, value_cache)


def shift(value, axis, step):
    n = lax.axis_size(axis)
    return lax.ppermute(value, axis, [(j, (j + step) % n) for j in range(n)])


def gather_axis(blocks, axis, stacked=True):
    n = lax.axis_size(axis)
    if n == 1:
        return blocks[None]
    if n == 2:
        return jnp.stack([blocks, shift(blocks, axis, 1)])
    assert n == 4
    from_prev = shift(blocks, axis, 1)
    from_next = shift(blocks, axis, -1)
    half = blocks.shape[-1] // 2
    far_a = shift(from_next[..., :half], axis, -1)
    far_b = shift(from_prev[..., half:], axis, 1)
    pieces = [blocks, from_next, (far_a, far_b), from_prev]
    return stack_pieces(pieces) if stacked else pieces


def stack_pieces(pieces):
    blocks, from_next, (far_a, far_b), from_prev = pieces
    far = jnp.concatenate([far_a, far_b], axis=-1)
    return jnp.stack([blocks, from_next, far, from_prev])


def exchange_slices(local_rows):
    yhi = lax.axis_index("yhi")
    core = lax.axis_index("core")
    own = yhi * 2 + core
    pick = lambda t: lax.dynamic_index_in_dim(local_rows, t, axis=1, keepdims=False)
    mine = pick(own)
    from_core = shift(pick(yhi * 2 + (1 - core)), "core", 1)
    from_yhi = shift(pick((1 - yhi) * 2 + core), "yhi", 1)
    diag = 3 - own
    from_diag = lax.ppermute(
        pick(diag), ("yhi", "core"), [(j, 3 - j) for j in range(4)]
    )
    parts = []
    for p in range(4):
        k = p ^ own
        parts.append(
            jnp.where(k == 0, mine, jnp.where(k == 1, from_core, jnp.where(k == 2, from_yhi, from_diag)))
        )
    return jnp.concatenate(parts, axis=0)


def gather_heads(attended):
    own = lax.axis_index("yhi") * 2 + lax.axis_index("core")
    across = shift(attended, "yhi", 1)
    side = shift(attended, "core", 1)
    diag = shift(across, "core", 1)
    parts = []
    for p in range(4):
        k = p ^ own
        parts.append(jnp.where(k == 0, attended, jnp.where(k == 1, side, jnp.where(k == 2, across, diag))))
    return jnp.concatenate(parts, axis=1)


def gather_pair(block):
    return gather_axis(block, "ylo")


def gather_first(paired):
    half = paired.shape[1] // 2
    return gather_axis(paired[:, :half], "x"), gather_axis(paired[:, half:], "z")


def gather_second(first):
    return gather_axis(first[0], "z", False), gather_axis(first[1], "x", False)


def relative_columns(values, rows):
    tokens = values.shape[0]
    nx, nz, nl = (lax.axis_size(a) for a in ROW_AXES)
    ix, iz, il = (lax.axis_index(a) for a in ROW_AXES)
    grid = values.reshape(tokens, nx, nz, nl, rows)
    grid = jnp.roll(grid, -ix, axis=1)
    grid = jnp.roll(grid, -iz, axis=2)
    grid = jnp.roll(grid, -il, axis=3)
    half = rows // 2
    part_a = jnp.transpose(grid[..., :half], (0, 2, 1, 3, 4)).reshape(tokens, -1)
    part_b = grid[..., half:].reshape(tokens, -1)
    return part_a, part_b


def project(parts, portions):
    portion_a, portion_b = (stack_pieces(p) for p in portions)
    cols = portion_a.shape[-1]
    part_a, part_b = parts
    first = jnp.dot(part_a, portion_a.reshape(-1, cols), preferred_element_type=jnp.float32)
    second = jnp.dot(part_b, portion_b.reshape(-1, cols), preferred_element_type=jnp.float32)
    return first + second


def layer(
    hidden_in,
    norm_gain,
    query_weight,
    key_weight,
    value_weight,
    out_weight,
    query_bias,
    key_bias,
    value_bias,
    span_start,
    span_length,
):
    slices = lax.axis_size(COL_AXES)
    token_rows = hidden_in.shape[0]
    local_spans = span_start.shape[0]
    span_size = token_rows // local_spans
    query_cols = query_weight.shape[1] // slices
    key_cols = key_weight.shape[1] // slices
    learner_rows = query_weight.shape[0]
    block_rows = slices * learner_rows
    joined = jnp.concatenate(
        [
            query_weight.reshape(learner_rows, slices, query_cols),
            key_weight.reshape(learner_rows, slices, key_cols),
            value_weight.reshape(learner_rows, slices, key_cols),
        ],
        axis=2,
    )
    qkv_paired = gather_pair(exchange_slices(joined))
    qkv_paired, out_weight, hidden_in = lax.optimization_barrier((qkv_paired, out_weight, hidden_in))
    qkv_portions = gather_second(gather_first(qkv_paired))
    out_rows_local = out_weight.shape[0]
    out_cols = out_weight.shape[1] // slices
    out_paired = gather_pair(exchange_slices(out_weight.reshape(out_rows_local, slices, out_cols)))
    qkv_portions, out_paired = lax.optimization_barrier((qkv_portions, out_paired))
    out_first = gather_first(out_paired)
    gathered = lax.all_gather(hidden_in, COL_AXES, axis=1, tiled=True)
    source = gathered.astype(jnp.float32)
    inverse_rms = lax.rsqrt(jnp.mean(source * source, axis=-1, keepdims=True) + epsilon)
    normed = (source * inverse_rms * norm_gain.astype(jnp.float32)).astype(jnp.bfloat16)
    normed_parts = relative_columns(normed, block_rows)
    projected = project(normed_parts, qkv_portions)
    out_portions = gather_second(out_first)
    query = projected[:, :query_cols] + query_bias.astype(jnp.float32)
    keys = projected[:, query_cols : query_cols + key_cols] + key_bias.astype(jnp.float32)
    values = projected[:, query_cols + key_cols :] + value_bias.astype(jnp.float32)
    local_heads = query_cols // HEAD
    local_kv = key_cols // HEAD
    groups = HEADS // KV_HEADS
    cosine, sine = angles(span_start, span_size)
    query = rotate(query.reshape(token_rows, local_heads, HEAD), cosine, sine).astype(jnp.bfloat16)
    keys = rotate(keys.reshape(token_rows, local_kv, HEAD), cosine, sine)
    live = (jnp.arange(span_size, dtype=jnp.int32)[None, :] < span_length[:, None]).reshape(
        token_rows, 1, 1
    )
    key_cache = jnp.where(live, keys, 0.0).astype(jnp.bfloat16)
    value_cache = jnp.where(live, values.reshape(token_rows, local_kv, HEAD), 0.0).astype(
        jnp.bfloat16
    )
    attended = attention(
        query.reshape(token_rows, local_heads * HEAD),
        key_cache.reshape(token_rows, local_kv * HEAD),
        value_cache.reshape(token_rows, local_kv * HEAD),
        span_length,
        span_size,
        groups,
    )
    all_heads = gather_heads(attended)
    combined = project(relative_columns(all_heads, block_rows), out_portions)
    attention_out = combined.astype(jnp.bfloat16)
    return (
        attention_out,
        key_cache.reshape(token_rows, local_kv * HEAD),
        value_cache.reshape(token_rows, local_kv * HEAD),
    )


def physical_mesh(mesh):
    members = mesh.shape["fsdp"]
    slices = mesh.shape["tensor"]
    shape = (4, members // 8, 2, slices // 2, 2)
    return Mesh(np.asarray(mesh.devices).reshape(shape), ROW_AXES + COL_AXES)


def solution(mesh):
    fine = physical_mesh(mesh)
    rows = ROW_AXES
    both = ROW_AXES + COL_AXES
    placed = (
        P(rows, COL_AXES),
        P(),
        P(both, None),
        P(both, None),
        P(both, None),
        P(both, None),
        P(COL_AXES),
        P(COL_AXES),
        P(COL_AXES),
        P(rows),
        P(rows),
    )
    return jax.shard_map(
        layer,
        mesh=fine,
        in_specs=placed,
        out_specs=(P(rows, COL_AXES), P(rows, COL_AXES), P(rows, COL_AXES)),
        check_vma=False,
    )
```
